32 devices in a mesh: groups: 2 (over y), seq: 4 (over z), dp: 4 (over x, core).
Axes of the slice: x: 2, y: 2, z: 4, core: 2. Of those that a mesh axis runs over, the one named last changes fastest.
Arguments:
- inputs: bfloat16 [8, 32768, 768], P(('groups', 'dp'), 'seq'), parts along dimension 0, may hold values from -33 to 33, as said below
- norm_gain: float32 [768], replicated, may hold values from 0.5 to 1.5
- inner_mix: bfloat16 [256, 256], replicated, may hold values from -0.375 to 0.375
- twiddle: float32 [128, 256], P('seq'), may hold values from 0.5 to 2
- outer_mix: bfloat16 [128, 128], replicated, may hold values from -0.5 to 0.5
- long_kernel: float32 [128, 256], P(None, 'seq'), may hold values from 0.5 to 2
- gate_weight: bfloat16 [768, 384], replicated, may hold values from -0.3125 to 0.3125
- out_weight: bfloat16 [768, 384], replicated, may hold values from -0.3125 to 0.3125
- cotangent: bfloat16 [8, 32768, 768], P(('groups', 'dp'), 'seq'), parts along dimension 0, may hold values from -6 to 6
Outputs:
- layer_out: bfloat16 [8, 32768, 768], P(('groups', 'dp'), 'seq'), parts along dimension 0
- input_grad: bfloat16 [8, 32768, 768], P(('groups', 'dp'), 'seq'), parts along dimension 0
- weight_grads: float32 [3072, 384], P(('groups', 'seq')), parts along dimension 0
The draws below stay inside these ranges and needn't reach their ends.
There are 2 independent parts, one for each index of `groups`. The reference program is written for one: setup_inputs(seed, part) draws one part's arguments, and reference() takes and returns one part's arrays. A program takes and returns all parts, laid end to end along the dimension named above; an argument that names none is the same for every part. Nothing has to cross between parts.
Inputs may be any that keep to these rules, and one draw needn't show every extreme that they name: `inputs`: activations' entries.
All inputs are finite; a program needn't handle non-finite values.
Results may differ from the reference program's by a relative error of at most 0.0072.
Values may be sent and summed in bfloat16 or wider, within the bound.
A program may use at most 384 MiB of HBM per device.

```python
import math
import jax
import jax.numpy as jnp
from jax import lax

OUTER = 128
INNER = 256
BLOCK = 384
CH_BLOCKS = 2
WIDTH = 768
LENGTH = 32768
BATCH = 4


def draw_inputs(key, part):
    key_vals, key_cols, key_rows = jax.random.split(key, 3)
    full_shape = (BATCH, LENGTH, WIDTH)
    col_scale = jnp.exp(jax.random.uniform(key_cols, (1, 1, WIDTH), jnp.float32, math.log(0.3), math.log(3.0)))
    values = jax.random.truncated_normal(key_vals, -4.0, 4.0, full_shape, jnp.float32)
    row_scale = jnp.exp(jax.random.uniform(key_rows, (BATCH, LENGTH, 1), jnp.float32, math.log(0.5), math.log(2.0)))
    return (values * row_scale * col_scale).astype(jnp.bfloat16)


def spiked(entries, rng, source, target, parts, factor):
    def block_of(axis_at):
        return (jnp.arange(entries.shape[axis_at]) // (entries.shape[axis_at] // parts)).reshape((-1,) + (1,) * (entries.ndim - 1 - axis_at))

    near = jax.random.permutation(rng, parts)[block_of(target)]
    other_side = (block_of(target) + parts // 2) % parts
    return jnp.where((block_of(source) == near) | (block_of(source) == other_side), factor * entries, entries)


def level_of(stream_key, dims, pieces, least, top_value):
    def one(axis_at, parts):
        steps = jax.random.uniform(jax.random.fold_in(jax.random.fold_in(stream_key, 6), axis_at), (parts,), jnp.float32, least / len(pieces), top_value / len(pieces))
        return jnp.repeat(jnp.exp(steps), dims[axis_at] // parts).reshape((-1,) + (1,) * (len(dims) - axis_at - 1))

    level = one(*pieces[0])
    for cut in pieces[1:]:
        level = level * one(*cut)
    return level


def normal_values(rng, shape, deviation, reach, cuts=(), kind=jnp.bfloat16):
    array = deviation * jax.random.normal(rng, shape, jnp.float32)
    if cuts:
        array = array * level_of(rng, shape, cuts, -0.22, 0.18)
    return jnp.clip(array, -reach, reach).astype(kind)


def noise_with(own_key, dims, scale, most, cuts, heavy, dtype=jnp.bfloat16):
    array = scale * jax.random.normal(own_key, dims, jnp.float32)
    if cuts:
        array = array * level_of(own_key, dims, cuts, -0.22, 0.18)
    return jnp.clip(spiked(array, jax.random.fold_in(own_key, 3), *heavy), -most, most).astype(dtype)


def setup_inputs(seed: int = 0, part: int = 0) -> dict:
    arg_keys = jax.random.split(jax.random.key(seed), 10)
    part_splits = jax.random.split(jax.random.fold_in(arg_keys[9], part), 10)
    return {
        "inputs": draw_inputs(jax.random.fold_in(jax.random.fold_in(arg_keys[9], part), 71), part),
        "norm_gain": jnp.clip(1.0 + 0.1 * jax.random.normal(arg_keys[1], (WIDTH,), jnp.float32), 0.5, 1.5),
        "inner_mix": normal_values(arg_keys[2], (INNER, INNER), INNER ** -0.5, 0.375),
        "twiddle": jnp.clip(jnp.exp(math.log(2.0) - 1.3862944 * jax.random.uniform(arg_keys[3], (OUTER, INNER), jnp.float32) ** level_of(arg_keys[3], (OUTER, INNER), ((0, 4),), -0.2, 0.2)), 0.5, 2.0),
        "outer_mix": normal_values(arg_keys[4], (OUTER, OUTER), OUTER ** -0.5, 0.5),
        "long_kernel": jnp.clip(jnp.exp(math.log(2.0) - 1.3862944 * jax.random.uniform(arg_keys[5], (OUTER, INNER), jnp.float32) ** level_of(arg_keys[5], (OUTER, INNER), ((1, 4),), -0.2, 0.2)), 0.5, 2.0),
        "gate_weight": normal_values(arg_keys[6], (CH_BLOCKS * BLOCK, BLOCK), BLOCK ** -0.5, 0.3125),
        "out_weight": normal_values(arg_keys[7], (CH_BLOCKS * BLOCK, BLOCK), BLOCK ** -0.5, 0.3125),
        "cotangent": noise_with(part_splits[8], (BATCH, LENGTH, WIDTH), 1.0, 6.0, ((0, 4), (1, 4)), (1, 2, 4, 2.0)),
    }


norm_eps = 1e-06

def widen(values):
    return lax.optimization_barrier(values).astype(jnp.float32)

def normalize(values, norm_gain):
    mean_square = lax.optimization_barrier(jnp.mean(values * values, axis=-1, keepdims=True))
    return values * lax.rsqrt(mean_square + norm_eps) * norm_gain

def block_apply(operand, weight):
    blocks = weight.shape[0] // weight.shape[1]
    grouped = widen(operand).reshape(operand.shape[0], blocks, weight.shape[1])
    stacked = weight.astype(jnp.float32).reshape(blocks, weight.shape[1], weight.shape[1])
    result = jnp.einsum('rki,kij->rkj', grouped, stacked)
    return result.reshape(operand.shape[0], -1)

def block_back(partner, weight):
    blocks = weight.shape[0] // weight.shape[1]
    grouped = widen(partner).reshape(partner.shape[0], blocks, weight.shape[1])
    stacked = weight.astype(jnp.float32).reshape(blocks, weight.shape[1], weight.shape[1])
    result = jnp.einsum('rkj,kij->rki', grouped, stacked)
    return result.reshape(partner.shape[0], -1)

def block_term(operand, partner):
    blocks = CH_BLOCKS
    grouped = widen(operand).reshape(operand.shape[0], blocks, BLOCK)
    other_rows = widen(partner).reshape(partner.shape[0], blocks, BLOCK)
    return jnp.einsum('rki,rkj->kij', grouped, other_rows).reshape(blocks * BLOCK, BLOCK)

def reference(inputs, norm_gain, inner_mix, twiddle, outer_mix, long_kernel, gate_weight, out_weight, cotangent):
    inner_wide = inner_mix.astype(jnp.float32)
    outer_wide = outer_mix.astype(jnp.float32)

    def one_sequence(carry, pair):
        seq_in, seq_cot = pair
        inputs_wide = seq_in.astype(jnp.float32)
        activation = normalize(inputs_wide, norm_gain).astype(jnp.bfloat16)
        grid_rows = widen(activation).reshape(OUTER, INNER, WIDTH)
        inner_out = jnp.einsum('jq,pqd->pjd', inner_wide, grid_rows)
        mixed_rows = (inner_out * twiddle[:, :, None]).astype(jnp.bfloat16)
        outer_out = jnp.einsum('ip,pjd->ijd', outer_wide, widen(mixed_rows))
        seq_mix = (outer_out * long_kernel[:, :, None]).astype(jnp.bfloat16).reshape(LENGTH, WIDTH)
        gate_pre = block_apply(activation, gate_weight)
        gate_sig = jax.nn.sigmoid(gate_pre)
        mix_wide = widen(seq_mix)
        gated_rows = (mix_wide * gate_pre * gate_sig).astype(jnp.bfloat16)
        layer_out = (inputs_wide + block_apply(gated_rows, out_weight)).astype(jnp.bfloat16)
        back_gated = block_back(seq_cot, out_weight)
        mix_grad = (back_gated * gate_pre * gate_sig).astype(jnp.bfloat16)
        gate_grad = (back_gated * mix_wide * gate_sig * (1.0 + gate_pre * (1.0 - gate_sig))).astype(jnp.bfloat16)
        act_grad = block_back(gate_grad, gate_weight)
        weight_term = jnp.concatenate([block_term(activation, gate_grad), block_term(gated_rows, seq_cot)], axis=0)
        scaled_back = (widen(mix_grad).reshape(OUTER, INNER, WIDTH) * long_kernel[:, :, None]).astype(jnp.bfloat16)
        back_outer = jnp.einsum('ip,ijd->pjd', outer_wide, widen(scaled_back)).astype(jnp.bfloat16)
        twisted = (widen(back_outer) * twiddle[:, :, None]).astype(jnp.bfloat16)
        inner_back = jnp.einsum('jq,pjd->pqd', inner_wide, widen(twisted))
        act_grad = act_grad + inner_back.reshape(LENGTH, WIDTH)
        pullback = jax.vjp(lambda wide_rows: normalize(wide_rows, norm_gain), inputs_wide)[1]
        input_grad = (seq_cot.astype(jnp.float32) + pullback(act_grad)[0]).astype(jnp.bfloat16)
        return (carry + weight_term, (layer_out, input_grad))
    start_term = jnp.zeros((2 * CH_BLOCKS * BLOCK, BLOCK), jnp.float32)
    total_term, (layer_out, input_grad) = lax.scan(one_sequence, start_term, (inputs, cotangent))
    weight_grads = total_term * (1.0 / math.sqrt(BATCH * LENGTH))
    return (layer_out, input_grad, weight_grads)
```

```python
import functools
import math

import jax
import jax.numpy as jnp
from jax import lax
from jax.experimental import pallas as pl
from jax.experimental.pallas import tpu as pltpu
from jax.sharding import PartitionSpec as P

norm_eps = 1e-06


def normalize(values, norm_gain):
    mean_square = jnp.mean(values * values, axis=-1, keepdims=True)
    return values * lax.rsqrt(mean_square + norm_eps) * norm_gain


def block_apply(operand, weight):
    blocks = weight.shape[0] // weight.shape[1]
    grouped = operand.reshape(operand.shape[0], blocks, weight.shape[1])
    stacked = weight.reshape(blocks, weight.shape[1], weight.shape[1])
    result = jnp.einsum("rki,kij->rkj", grouped, stacked, preferred_element_type=jnp.float32)
    return result.reshape(operand.shape[0], -1)


def block_back(partner, weight):
    blocks = weight.shape[0] // weight.shape[1]
    grouped = partner.reshape(partner.shape[0], blocks, weight.shape[1])
    stacked = weight.reshape(blocks, weight.shape[1], weight.shape[1])
    result = jnp.einsum("rkj,kij->rki", grouped, stacked, preferred_element_type=jnp.float32)
    return result.reshape(partner.shape[0], -1)


def block_term(operand, partner, blocks, block_size):
    grouped = operand.reshape(operand.shape[0], blocks, block_size)
    other_rows = partner.reshape(partner.shape[0], blocks, block_size)
    result = jnp.einsum("rki,rkj->kij", grouped, other_rows, preferred_element_type=jnp.float32)
    return result.reshape(blocks * block_size, block_size)


def to_columns(row_layout):
    return lax.all_to_all(row_layout, "seq", split_axis=2, concat_axis=1, tiled=True)


def to_rows(col_layout):
    return lax.all_to_all(col_layout, "seq", split_axis=1, concat_axis=2, tiled=True)


def shards_plain(
    inputs,
    norm_gain,
    inner_mix,
    twiddle,
    outer_mix,
    long_kernel,
    gate_weight,
    out_weight,
    cotangent,
):
    batch_local, rows_local, channels = inputs.shape
    inner_len = inner_mix.shape[0]
    local_outer = rows_local // inner_len
    flat_rows = batch_local * rows_local
    block_size = gate_weight.shape[1]
    blocks = gate_weight.shape[0] // block_size
    all_tokens = batch_local * lax.axis_size("dp") * rows_local * lax.axis_size("seq")
    grad_scale = 1.0 / math.sqrt(all_tokens)
    inputs_wide = inputs.reshape(flat_rows, channels).astype(jnp.float32)
    activation = normalize(inputs_wide, norm_gain).astype(jnp.bfloat16)
    grid_rows = activation.reshape(batch_local, local_outer, inner_len, channels)
    inner_out = jnp.einsum(
        "jq,bpqd->bpjd", inner_mix, grid_rows, preferred_element_type=jnp.float32
    )
    mixed_rows = (inner_out * twiddle[None, :, :, None]).astype(jnp.bfloat16)
    columns = to_columns(mixed_rows)
    outer_out = jnp.einsum("ip,bpjd->bijd", outer_mix, columns, preferred_element_type=jnp.float32)
    mixed_cols = (outer_out * long_kernel[None, :, :, None]).astype(jnp.bfloat16)
    seq_mix = to_rows(mixed_cols).reshape(flat_rows, channels)
    gate_pre = block_apply(activation, gate_weight)
    gate_sig = jax.nn.sigmoid(gate_pre)
    mix_wide = seq_mix.astype(jnp.float32)
    gated_rows = (mix_wide * gate_pre * gate_sig).astype(jnp.bfloat16)
    layer_out = (inputs_wide + block_apply(gated_rows, out_weight)).astype(jnp.bfloat16)
    cotan_rows = cotangent.reshape(flat_rows, channels)
    back_gated = block_back(cotan_rows, out_weight)
    mix_grad = (back_gated * gate_pre * gate_sig).astype(jnp.bfloat16)
    gate_grad = (back_gated * mix_wide * gate_sig * (1.0 + gate_pre * (1.0 - gate_sig))).astype(
        jnp.bfloat16
    )
    act_grad = block_back(gate_grad, gate_weight)
    weight_term = jnp.concatenate(
        [
            block_term(activation, gate_grad, blocks, block_size),
            block_term(gated_rows, cotan_rows, blocks, block_size),
        ],
        axis=0,
    )
    grad_cols = to_columns(mix_grad.reshape(batch_local, local_outer, inner_len, channels))
    scaled_back = (grad_cols.astype(jnp.float32) * long_kernel[None, :, :, None]).astype(
        jnp.bfloat16
    )
    back_outer = jnp.einsum(
        "ip,bijd->bpjd", outer_mix, scaled_back, preferred_element_type=jnp.float32
    ).astype(jnp.bfloat16)
    back_rows = to_rows(back_outer)
    twisted = (back_rows.astype(jnp.float32) * twiddle[None, :, :, None]).astype(jnp.bfloat16)
    inner_back = jnp.einsum("jq,bpjd->bpqd", inner_mix, twisted, preferred_element_type=jnp.float32)
    act_grad = act_grad + inner_back.reshape(flat_rows, channels)
    pullback = jax.vjp(lambda wide_rows: normalize(wide_rows, norm_gain), inputs_wide)[1]
    input_grad = (cotan_rows.astype(jnp.float32) + pullback(act_grad)[0]).astype(jnp.bfloat16)
    shard_term = lax.psum_scatter(weight_term, "seq", scatter_dimension=0, tiled=True)
    weight_grads = lax.psum(shard_term, "dp") * grad_scale
    return (layer_out.reshape(inputs.shape), input_grad.reshape(inputs.shape), weight_grads)


def dot(lhs, rhs, lhs_dim=1, rhs_dim=0):
    return lax.dot_general(
        lhs, rhs, (((lhs_dim,), (rhs_dim,)), ((), ())), preferred_element_type=jnp.float32
    )


def row_scale(wide):
    return lax.rsqrt(jnp.sum(wide * wide, axis=-1, keepdims=True) / wide.shape[-1] + norm_eps)


def pick_column(table, at):
    lanes = lax.broadcasted_iota(jnp.int32, table.shape, 1)
    return jnp.sum(jnp.where(lanes == at, table, 0.0), axis=-1, keepdims=True)


def normed(rows, gain):
    wide = rows.astype(jnp.float32)
    return (wide * row_scale(wide) * gain).astype(jnp.bfloat16)


def gate_terms(act, weight):
    gate_pre = dot(act, weight)
    gate_sig = jax.nn.sigmoid(gate_pre)
    return gate_pre, gate_sig


SUB = 16


def layer_kernel(
    grad_scale,
    gain_ref,
    inner_ref,
    twiddle_ref,
    outer_ref,
    kernel_ref,
    gate_ref,
    out_ref,
    x_hbm,
    cot_hbm,
    layer_hbm,
    input_grad_hbm,
    weight_hbm,
    grad_hbm,
    mixed_hbm,
    scaled_hbm,
    seq_hbm,
    back_hbm,
    first_buf,
    second_buf,
    wide_outer,
    block_buf,
    x_buf,
    cot_buf,
    grad_buf,
    swap_buf,
    result_buf,
    inner_t_buf,
    term_buf,
    share_buf,
    piece_buf,
    piece_in_buf,
    final_buf,
    load_sem,
    store_sem,
    own_sem,
    send_sem,
    in_sem,
    row_sem,
    back_sem,
    weight_send_sem,
    weight_sem,
):
    seq_n, rows, cols, channels = first_buf.shape
    dp_n = share_buf.shape[0]
    outer_len = seq_n * rows
    inner_len = seq_n * cols
    size = gate_ref.shape[1]
    blocks = channels // size
    part_cols = block_buf.shape[-1]
    lane_parts = channels // part_cols
    me = lax.axis_index("seq")
    my_dp = lax.axis_index("dp")
    gain = gain_ref[...]
    bf16 = jnp.bfloat16

    def seq_peer(step):
        return lax.rem(me + step, seq_n)

    def dp_peer(step):
        return lax.rem(my_dp + step, dp_n)

    def remote(source, target, send, receive, axis, index):
        return pltpu.make_async_remote_copy(
            src_ref=source,
            dst_ref=target,
            send_sem=send,
            recv_sem=receive,
            device_id={axis: index},
            device_id_type=pl.DeviceIdType.MESH,
        )

    def load(sem, source, target):
        copy = pltpu.make_async_copy(source, target, load_sem.at[sem])
        copy.start()
        return copy

    def store(sem, source, target):
        copy = pltpu.make_async_copy(source, target, store_sem.at[sem])
        copy.start()
        return copy

    def row_send(buf, target, send, receive, row):
        for step in range(1, seq_n):
            peer = seq_peer(step)
            remote(buf.at[peer, row], target.at[me, row], send, receive, "seq", peer).start()

    others = pl.ds(0, seq_n - 1)

    def wait_all(buf, target, send, receive):
        copy = remote(buf.at[others], target.at[others], send, receive, "seq", seq_peer(1))
        if receive is not None:
            copy.wait_recv()
        return copy

    x_first = load(0, x_hbm.at[0], x_buf)
    barrier = pltpu.get_barrier_semaphore()
    for step in range(1, seq_n):
        pl.semaphore_signal(
            barrier, 1, device_id={"seq": seq_peer(step)}, device_id_type=pl.DeviceIdType.MESH
        )
    for step in range(1, dp_n):
        pl.semaphore_signal(
            barrier, 1, device_id={"dp": dp_peer(step)}, device_id_type=pl.DeviceIdType.MESH
        )
    pl.semaphore_wait(barrier, seq_n + dp_n - 2)
    x_first.wait()

    def enter_row(row, carry):
        load(0, x_hbm.at[row], x_buf).wait()
        act = normed(x_buf[...], gain)
        mixed = dot(inner_ref[...], act) * pick_column(twiddle_ref[...], row)
        first_buf[:, pl.ds(row, 1)] = mixed.astype(bf16).reshape(seq_n, 1, cols, channels)
        row_send(first_buf, mixed_hbm, send_sem.at[0], in_sem.at[0], row)
        return carry

    lax.fori_loop(0, rows, enter_row, 0)
    mixed_own = pltpu.make_async_copy(first_buf.at[me], mixed_hbm.at[me], own_sem.at[0])
    mixed_own.start()

    def grad_row(row, carry):
        loads = [load(0, x_hbm.at[row], x_buf), load(1, cot_hbm.at[row], cot_buf)]
        for copy in loads:
            copy.wait()
        act = normed(x_buf[...], gain)
        for k in range(blocks):
            part = slice(k * size, (k + 1) * size)
            gate_pre, gate_sig = gate_terms(act[:, part], gate_ref[part, :])
            back = dot(cot_buf[:, part], out_ref[part, :], 1, 1)
            grad = (back * gate_pre * gate_sig).astype(bf16)
            second_buf[:, pl.ds(row, 1), :, part] = grad.reshape(seq_n, 1, cols, size)
        row_send(second_buf, scaled_hbm, send_sem.at[1], in_sem.at[1], row)
        return carry

    lax.fori_loop(0, rows, grad_row, 0)
    scaled_own = pltpu.make_async_copy(second_buf.at[me], scaled_hbm.at[me], own_sem.at[1])
    scaled_own.start()

    tile = SUB * SUB
    tiles = outer_len // SUB

    def widen_outer(transposed):
        def one(at, carry):
            shape = (tile, outer_len)
            i_of = (lax.broadcasted_iota(jnp.int32, shape, 0) >> 4) + at * SUB
            pick = (i_of == lax.broadcasted_iota(jnp.int32, shape, 1)).astype(bf16)
            picked = dot(pick, outer_ref[...], 1, 1 if transposed else 0).astype(bf16)
            shape = (outer_len, outer_len * SUB)
            p_of = lax.broadcasted_iota(jnp.int32, shape, 1) >> 4
            spread = (p_of == lax.broadcasted_iota(jnp.int32, shape, 0)).astype(bf16)
            full = dot(picked, spread)
            shape = full.shape
            low = lax.broadcasted_iota(jnp.int32, shape, 0) & (SUB - 1)
            high = lax.broadcasted_iota(jnp.int32, shape, 1) & (SUB - 1)
            at_row = pl.multiple_of(at * tile, tile)
            wide_outer[pl.ds(at_row, tile), :] = jnp.where(low == high, full, 0.0).astype(bf16)
            return carry

        lax.fori_loop(0, tiles, one, 0)

    def kernel_column(at, group):
        at_row = pl.multiple_of(at * SUB, SUB)
        table = kernel_ref[pl.ds(at_row, SUB), :]
        spread = jnp.broadcast_to(table[:, None, :], (SUB, SUB, cols)).reshape(tile, cols)
        wanted = (lax.broadcasted_iota(jnp.int32, spread.shape, 0) & (SUB - 1)) + group * SUB
        lanes = lax.broadcasted_iota(jnp.int32, spread.shape, 1)
        return jnp.sum(jnp.where(lanes == wanted, spread, 0.0), axis=-1, keepdims=True)

    tiles_each = rows // SUB

    def mix_outer(source, target, forward):
        def one_block(at, carry):
            group = at // lane_parts
            sub_rows = pl.ds(pl.multiple_of(group * SUB, SUB), SUB)
            lanes = pl.ds(pl.multiple_of((at % lane_parts) * part_cols, part_cols), part_cols)
            load(0, source.at[:, :, sub_rows, lanes], block_buf).wait()

            def whole_of(i):
                return i // tiles_each, pl.ds((i % tiles_each) * SUB, SUB)

            if not forward:

                def scale_tile(i, carry):
                    owner, inside = whole_of(i)
                    held = block_buf[owner, inside].reshape(tile, part_cols).astype(jnp.float32)
                    scaled = (held * kernel_column(i, group)).astype(bf16)
                    block_buf[owner, inside] = scaled.reshape(SUB, SUB, part_cols)
                    return carry

                lax.fori_loop(0, tiles, scale_tile, 0)

            def one_tile(i, carry):
                at_row = pl.multiple_of(i * tile, tile)
                block = block_buf[...].reshape(outer_len * SUB, part_cols)
                mixed = dot(wide_outer[pl.ds(at_row, tile), :], block)
                if forward:
                    mixed = mixed * kernel_column(i, group)
                owner, inside = whole_of(i)
                target[owner, inside, sub_rows, lanes] = mixed.astype(bf16).reshape(
                    SUB, SUB, part_cols
                )
                return carry

            lax.fori_loop(0, tiles, one_tile, 0)
            return carry

        lax.fori_loop(0, cols // SUB * lane_parts, one_block, 0)

    widen_outer(False)
    eye_shape = (inner_len, inner_len)
    eye = lax.broadcasted_iota(jnp.int32, eye_shape, 0) == lax.broadcasted_iota(
        jnp.int32, eye_shape, 1
    )
    inner_t_buf[...] = dot(eye.astype(bf16), inner_ref[...], 1, 1).astype(bf16)

    mixed_own.wait()
    wait_all(first_buf, mixed_hbm, send_sem.at[0], in_sem.at[0]).wait_send()
    mix_outer(mixed_hbm, first_buf, True)

    def seq_send(row, carry):
        row_send(first_buf, seq_hbm, send_sem.at[2], row_sem.at[row], row)
        return carry

    lax.fori_loop(0, rows, seq_send, 0)
    seq_own = pltpu.make_async_copy(first_buf.at[me], seq_hbm.at[me], own_sem.at[0])
    seq_own.start()
    widen_outer(True)

    scaled_own.wait()
    wait_all(second_buf, scaled_hbm, send_sem.at[1], in_sem.at[1]).wait_send()
    mix_outer(scaled_hbm, second_buf, False)

    def back_send(row, carry):
        row_send(second_buf, back_hbm, send_sem.at[3], back_sem.at[row], row)
        return carry

    ahead = max(rows // 4, 1)
    lax.fori_loop(0, ahead, back_send, 0)
    back_own = pltpu.make_async_copy(second_buf.at[me], back_hbm.at[me], own_sem.at[1])
    back_own.start()

    term_buf[...] = jnp.zeros_like(term_buf)
    seq_own.wait()

    def take_row(source, receive, row):
        remote(
            first_buf.at[others, row],
            source.at[others, row],
            send_sem.at[2],
            receive.at[row],
            "seq",
            seq_peer(1),
        ).wait_recv()
        load(3, source.at[:, row], swap_buf).wait()

    def gate_row(row, carry):
        loads = [load(0, x_hbm.at[row], x_buf), load(1, cot_hbm.at[row], cot_buf)]
        take_row(seq_hbm, row_sem, row)
        for copy in loads:
            copy.wait()
        all_act = normed(x_buf[...], gain)
        for k in range(blocks):
            part = slice(k * size, (k + 1) * size)
            act = all_act[:, part]
            cot = cot_buf[:, part]
            gate_pre, gate_sig = gate_terms(act, gate_ref[part, :])
            mix = swap_buf[:, :, part].reshape(inner_len, size).astype(jnp.float32)
            gated = (mix * gate_pre * gate_sig).astype(bf16)
            result_buf[:, part] = (
                x_buf[:, part].astype(jnp.float32) + dot(gated, out_ref[part, :])
            ).astype(bf16)
            back = dot(cot, out_ref[part, :], 1, 1)
            grad = (back * mix * gate_sig * (1.0 + gate_pre * (1.0 - gate_sig))).astype(bf16)
            grad_buf[:, part] = grad
            held = term_buf.shape[1:]
            term_buf[k] += dot(act, grad, 0, 0).reshape(held)
            term_buf[blocks + k] += dot(gated, cot, 0, 0).reshape(held)
        stores = [
            store(0, result_buf, layer_hbm.at[row]),
            store(1, grad_buf, grad_hbm.at[row]),
        ]
        for copy in stores:
            copy.wait()
        return carry

    lax.fori_loop(0, rows, gate_row, 0)

    def share_copy(step):
        peer = dp_peer(step)
        return remote(
            term_buf.at[:, peer],
            share_buf.at[my_dp],
            weight_send_sem.at[0, step],
            weight_sem.at[0, step],
            "dp",
            peer,
        )

    def piece_copy(step):
        peer = seq_peer(step)
        return remote(
            piece_buf.at[peer],
            piece_in_buf.at[me],
            weight_send_sem.at[1, step],
            weight_sem.at[1, step],
            "seq",
            peer,
        )

    def final_copy(step):
        peer = dp_peer(step)
        return remote(
            final_buf,
            weight_hbm.at[my_dp],
            weight_send_sem.at[2, step],
            weight_sem.at[2, step],
            "dp",
            peer,
        )

    final_own = pltpu.make_async_copy(final_buf, weight_hbm.at[my_dp], own_sem.at[2])
    for step in range(1, dp_n):
        share_copy(step).start()
    back_own.wait()

    def leave_row(row, carry):
        loads = [
            load(0, x_hbm.at[row], x_buf),
            load(1, cot_hbm.at[row], cot_buf),
            load(2, grad_hbm.at[row], grad_buf),
        ]

        @pl.when(row + ahead < rows)
        def _():
            back_send(row + ahead, 0)

        @pl.when(row == rows // 3)
        def _():
            for step in range(1, dp_n):
                share_copy(step).wait()
            share_buf[my_dp] = term_buf[:, my_dp]
            total = share_buf[0]
            for t in range(1, dp_n):
                total += share_buf[t]
            piece_buf[...] = total.astype(piece_buf.dtype)
            final_buf[...] = jnp.zeros_like(final_buf)
            for s in range(seq_n):
                final_buf[...] += jnp.where(me == s, total[s], 0.0)
            for step in range(1, seq_n):
                piece_copy(step).start()

        @pl.when(row == 2 * rows // 3)
        def _():
            for step in range(1, seq_n):
                piece_copy(step).wait()
            total = final_buf[...]
            for step in range(1, seq_n):
                total += piece_in_buf[seq_peer(step)].astype(jnp.float32)
            final_buf[...] = total * grad_scale
            final_own.start()
            for step in range(1, dp_n):
                final_copy(step).start()

        for copy in loads:
            copy.wait()
        take_row(back_hbm, back_sem, row)
        column = pick_column(twiddle_ref[...], row)
        parts = []
        for k in range(blocks):
            part = slice(k * size, (k + 1) * size)
            held = swap_buf[:, :, part].reshape(inner_len, size).astype(jnp.float32)
            twisted = (held * column).astype(bf16)
            parts.append(
                dot(grad_buf[:, part], gate_ref[part, :], 1, 1) + dot(inner_t_buf[...], twisted)
            )
        act_grad = jnp.concatenate(parts, axis=1)
        wide = x_buf[...].astype(jnp.float32)
        scale = row_scale(wide)
        pulled = act_grad * gain
        share = jnp.sum(pulled * wide, axis=-1, keepdims=True) / channels
        grad = pulled * scale - wide * (scale * scale * scale * share)
        result_buf[...] = (cot_buf[...].astype(jnp.float32) + grad).astype(bf16)
        store(0, result_buf, input_grad_hbm.at[row]).wait()
        return carry

    lax.fori_loop(0, rows, leave_row, 0)
    final_own.wait()
    for step in range(1, dp_n):
        final_copy(step).wait()
    wait_all(first_buf, seq_hbm, send_sem.at[2], None).wait_send()
    wait_all(second_buf, back_hbm, send_sem.at[3], None).wait_send()


def shards_fast(
    inputs,
    norm_gain,
    inner_mix,
    twiddle,
    outer_mix,
    long_kernel,
    gate_weight,
    out_weight,
    cotangent,
):
    _, rows_local, channels = inputs.shape
    inner_len = inner_mix.shape[0]
    outer_len = outer_mix.shape[0]
    rows = rows_local // inner_len
    size = gate_weight.shape[1]
    blocks = gate_weight.shape[0] // size
    seq_n = lax.axis_size("seq")
    dp_n = lax.axis_size("dp")
    cols = inner_len // seq_n
    piece = size // dp_n
    grad_scale = 1.0 / math.sqrt(dp_n * rows_local * seq_n)
    bf16 = jnp.bfloat16
    f32 = jnp.float32
    part_cols = channels // 2

    row_shape = jax.ShapeDtypeStruct((rows, inner_len, channels), bf16)
    swap_shape = jax.ShapeDtypeStruct((seq_n, rows, cols, channels), bf16)
    held = pl.BlockSpec(memory_space=pltpu.VMEM)
    anywhere = pl.BlockSpec(memory_space=pl.ANY)
    row_buf = pltpu.VMEM((inner_len, channels), bf16)
    sems = pltpu.SemaphoreType.DMA

    layer_out, input_grad, weight_grads = pl.pallas_call(
        functools.partial(layer_kernel, grad_scale),
        in_specs=[held] * 7 + [anywhere] * 2,
        out_specs=[anywhere] * 8,
        out_shape=[
            row_shape,
            row_shape,
            jax.ShapeDtypeStruct((dp_n, piece, size), f32),
            row_shape,
        ]
        + [swap_shape] * 4,
        scratch_shapes=[
            pltpu.VMEM(swap_shape.shape, bf16),
            pltpu.VMEM(swap_shape.shape, bf16),
            pltpu.VMEM((outer_len * SUB, outer_len * SUB), bf16),
            pltpu.VMEM((seq_n, rows, SUB, part_cols), bf16),
            row_buf,
            row_buf,
            row_buf,
            pltpu.VMEM((seq_n, cols, channels), bf16),
            row_buf,
            pltpu.VMEM((inner_len, inner_len), bf16),
            pltpu.VMEM((seq_n, dp_n, piece, size), f32),
            pltpu.VMEM((dp_n, seq_n, piece, size), f32),
            pltpu.VMEM((seq_n, piece, size), bf16),
            pltpu.VMEM((seq_n, piece, size), bf16),
            pltpu.VMEM((piece, size), f32),
            sems((4,)),
            sems((2,)),
            sems((3,)),
            sems((4,)),
            sems((2,)),
            sems((rows,)),
            sems((rows,)),
            sems((3, max(seq_n, dp_n))),
            sems((3, max(seq_n, dp_n))),
        ],
        compiler_params=pltpu.CompilerParams(
            collective_id=0, has_side_effects=True, vmem_limit_bytes=60 * 2**20
        ),
        cost_estimate=pl.CostEstimate(
            flops=24 * rows_local * channels * size,
            bytes_accessed=40 * rows_local * channels,
            transcendentals=0,
        ),
        name="layer",
    )(
        norm_gain.reshape(1, channels),
        inner_mix,
        twiddle.T,
        outer_mix,
        long_kernel,
        gate_weight,
        out_weight,
        inputs.reshape(row_shape.shape),
        cotangent.reshape(row_shape.shape),
    )[:3]
    return (
        layer_out.reshape(inputs.shape),
        input_grad.reshape(inputs.shape),
        weight_grads.reshape(dp_n * piece, size),
    )


def shards(*arrays):
    batch, rows_local, channels = arrays[0].shape
    inner_len = arrays[2].shape[0]
    cols = arrays[5].shape[1]
    size = arrays[6].shape[1]
    blocks = arrays[6].shape[0] // size
    seq_n, dp_n = lax.axis_size("seq"), lax.axis_size("dp")
    fits = (
        batch == 1
        and min(seq_n, dp_n) > 1
        and rows_local // inner_len % SUB == 0
        and cols % SUB == 0
        and channels % 256 == 0
        and size % 128 == 0
        and 2 * blocks == seq_n
        and size % (16 * dp_n) == 0
        and inner_len % 128 == 0
    )
    if fits:
        return shards_fast(*arrays)
    return shards_plain(*arrays)


def solution(mesh):
    return jax.shard_map(
        shards,
        mesh=mesh,
        in_specs=(
            P(("groups", "dp"), "seq", None),
            P(),
            P(),
            P("seq", None),
            P(),
            P(None, "seq"),
            P(),
            P(),
            P(("groups", "dp"), "seq", None),
        ),
        out_specs=(
            P(("groups", "dp"), "seq", None),
            P(("groups", "dp"), "seq", None),
            P(("groups", "seq"), None),
        ),
        check_vma=False,
    )
```

```python
import functools
import math

import jax
import jax.numpy as jnp
from jax import lax
from jax.experimental import pallas as pl
from jax.experimental.pallas import tpu as pltpu
from jax.sharding import PartitionSpec as P

norm_eps = 1e-06


def normalize(values, norm_gain):
    mean_square = jnp.mean(values * values, axis=-1, keepdims=True)
    return values * lax.rsqrt(mean_square + norm_eps) * norm_gain


def block_apply(operand, weight):
    blocks = weight.shape[0] // weight.shape[1]
    grouped = operand.reshape(operand.shape[0], blocks, weight.shape[1])
    stacked = weight.reshape(blocks, weight.shape[1], weight.shape[1])
    result = jnp.einsum("rki,kij->rkj", grouped, stacked, preferred_element_type=jnp.float32)
    return result.reshape(operand.shape[0], -1)


def block_back(partner, weight):
    blocks = weight.shape[0] // weight.shape[1]
    grouped = partner.reshape(partner.shape[0], blocks, weight.shape[1])
    stacked = weight.reshape(blocks, weight.shape[1], weight.shape[1])
    result = jnp.einsum("rkj,kij->rki", grouped, stacked, preferred_element_type=jnp.float32)
    return result.reshape(partner.shape[0], -1)


def block_term(operand, partner, blocks, block_size):
    grouped = operand.reshape(operand.shape[0], blocks, block_size)
    other_rows = partner.reshape(partner.shape[0], blocks, block_size)
    result = jnp.einsum("rki,rkj->kij", grouped, other_rows, preferred_element_type=jnp.float32)
    return result.reshape(blocks * block_size, block_size)


def to_columns(row_layout):
    return lax.all_to_all(row_layout, "seq", split_axis=2, concat_axis=1, tiled=True)


def to_rows(col_layout):
    return lax.all_to_all(col_layout, "seq", split_axis=1, concat_axis=2, tiled=True)


def shards_plain(
    inputs,
    norm_gain,
    inner_mix,
    twiddle,
    outer_mix,
    long_kernel,
    gate_weight,
    out_weight,
    cotangent,
):
    batch_local, rows_local, channels = inputs.shape
    inner_len = inner_mix.shape[0]
    local_outer = rows_local // inner_len
    flat_rows = batch_local * rows_local
    block_size = gate_weight.shape[1]
    blocks = gate_weight.shape[0] // block_size
    all_tokens = batch_local * lax.axis_size("dp") * rows_local * lax.axis_size("seq")
    grad_scale = 1.0 / math.sqrt(all_tokens)
    inputs_wide = inputs.reshape(flat_rows, channels).astype(jnp.float32)
    activation = normalize(inputs_wide, norm_gain).astype(jnp.bfloat16)
    grid_rows = activation.reshape(batch_local, local_outer, inner_len, channels)
    inner_out = jnp.einsum(
        "jq,bpqd->bpjd", inner_mix, grid_rows, preferred_element_type=jnp.float32
    )
    mixed_rows = (inner_out * twiddle[None, :, :, None]).astype(jnp.bfloat16)
    columns = to_columns(mixed_rows)
    outer_out = jnp.einsum("ip,bpjd->bijd", outer_mix, columns, preferred_element_type=jnp.float32)
    mixed_cols = (outer_out * long_kernel[None, :, :, None]).astype(jnp.bfloat16)
    seq_mix = to_rows(mixed_cols).reshape(flat_rows, channels)
    gate_pre = block_apply(activation, gate_weight)
    gate_sig = jax.nn.sigmoid(gate_pre)
    mix_wide = seq_mix.astype(jnp.float32)
    gated_rows = (mix_wide * gate_pre * gate_sig).astype(jnp.bfloat16)
    layer_out = (inputs_wide + block_apply(gated_rows, out_weight)).astype(jnp.bfloat16)
    cotan_rows = cotangent.reshape(flat_rows, channels)
    back_gated = block_back(cotan_rows, out_weight)
    mix_grad = (back_gated * gate_pre * gate_sig).astype(jnp.bfloat16)
    gate_grad = (back_gated * mix_wide * gate_sig * (1.0 + gate_pre * (1.0 - gate_sig))).astype(
        jnp.bfloat16
    )
    act_grad = block_back(gate_grad, gate_weight)
    weight_term = jnp.concatenate(
        [
            block_term(activation, gate_grad, blocks, block_size),
            block_term(gated_rows, cotan_rows, blocks, block_size),
        ],
        axis=0,
    )
    grad_cols = to_columns(mix_grad.reshape(batch_local, local_outer, inner_len, channels))
    scaled_back = (grad_cols.astype(jnp.float32) * long_kernel[None, :, :, None]).astype(
        jnp.bfloat16
    )
    back_outer = jnp.einsum(
        "ip,bijd->bpjd", outer_mix, scaled_back, preferred_element_type=jnp.float32
    ).astype(jnp.bfloat16)
    back_rows = to_rows(back_outer)
    twisted = (back_rows.astype(jnp.float32) * twiddle[None, :, :, None]).astype(jnp.bfloat16)
    inner_back = jnp.einsum("jq,bpjd->bpqd", inner_mix, twisted, preferred_element_type=jnp.float32)
    act_grad = act_grad + inner_back.reshape(flat_rows, channels)
    pullback = jax.vjp(lambda wide_rows: normalize(wide_rows, norm_gain), inputs_wide)[1]
    input_grad = (cotan_rows.astype(jnp.float32) + pullback(act_grad)[0]).astype(jnp.bfloat16)
    shard_term = lax.psum_scatter(weight_term, "seq", scatter_dimension=0, tiled=True)
    weight_grads = lax.psum(shard_term, "dp") * grad_scale
    return (layer_out.reshape(inputs.shape), input_grad.reshape(inputs.shape), weight_grads)


def dot(lhs, rhs, lhs_dim=1, rhs_dim=0):
    return lax.dot_general(
        lhs, rhs, (((lhs_dim,), (rhs_dim,)), ((), ())), preferred_element_type=jnp.float32
    )


def row_scale(wide):
    return lax.rsqrt(jnp.sum(wide * wide, axis=-1, keepdims=True) / wide.shape[-1] + norm_eps)


def pick_column(table, at):
    lanes = lax.broadcasted_iota(jnp.int32, table.shape, 1)
    return jnp.sum(jnp.where(lanes == at, table, 0.0), axis=-1, keepdims=True)


def normed(rows, gain):
    wide = rows.astype(jnp.float32)
    return (wide * row_scale(wide) * gain).astype(jnp.bfloat16)


def gate_terms(act, weight):
    gate_pre = dot(act, weight)
    gate_sig = jax.nn.sigmoid(gate_pre)
    return gate_pre, gate_sig


SUB = 16


def layer_kernel(
    grad_scale,
    gain_ref,
    inner_ref,
    twiddle_ref,
    outer_ref,
    kernel_ref,
    gate_hbm,
    out_hbm,
    x_hbm,
    cot_hbm,
    first_buf,
    second_buf,
    weight_hbm,
    layer_hbm,
    grad_hbm,
    mixed_hbm,
    scaled_hbm,
    seq_hbm,
    back_hbm,
    twiddle_t_buf,
    kernel_buf,
    gate_buf,
    out_buf,
    wide_outer,
    block_buf,
    x_buf,
    cot_buf,
    grad_buf,
    swap_buf,
    result_buf,
    inner_t_buf,
    term_buf,
    share_buf,
    total_buf,
    piece_buf,
    piece_in_buf,
    final_buf,
    load_sem,
    store_sem,
    own_sem,
    send_sem,
    in_sem,
    row_sem,
    back_sem,
    back_send_sem,
    layer_sem,
    weight_send_sem,
    weight_sem,
):
    rows, seq_n, cols, channels = first_buf.shape
    dp_n = share_buf.shape[0]
    outer_len = seq_n * rows
    inner_len = seq_n * cols
    size = gate_buf.shape[1]
    blocks = channels // size
    part_cols = block_buf.shape[-1]
    lane_parts = channels // part_cols
    me = lax.axis_index("seq")
    my_dp = lax.axis_index("dp")
    gain = gain_ref[...].reshape(1, channels)
    bf16 = jnp.bfloat16

    def seq_peer(step):
        return lax.rem(me + step, seq_n)

    def dp_peer(step):
        return lax.rem(my_dp + step, dp_n)

    def remote(source, target, send, receive, axis, index):
        return pltpu.make_async_remote_copy(
            src_ref=source,
            dst_ref=target,
            send_sem=send,
            recv_sem=receive,
            device_id={axis: index},
            device_id_type=pl.DeviceIdType.MESH,
        )

    def load(sem, source, target):
        copy = pltpu.make_async_copy(source, target, load_sem.at[sem])
        copy.start()
        return copy

    def store(sem, source, target):
        copy = pltpu.make_async_copy(source, target, store_sem.at[sem])
        copy.start()
        return copy

    def row_send(buf, target, send, receive, row):
        for step in range(1, seq_n):
            peer = seq_peer(step)
            remote(buf.at[row, peer], target.at[me, row], send, receive, "seq", peer).start()

    others = pl.ds(0, seq_n - 1)

    def whole(target, send, receive):
        return remote(target.at[others], target.at[others], send, receive, "seq", seq_peer(1))

    def one_row(target, send, receive, row):
        held = target.at[others, row]
        return remote(held, held, send, receive, "seq", seq_peer(1))

    x_first = load(0, x_hbm.at[0], x_buf)
    weights = [load(2, gate_hbm, gate_buf), load(3, out_hbm, out_buf)]
    twiddle_t_buf[...] = twiddle_ref[...].T
    kernel_buf[...] = kernel_ref[...].T
    barrier = pltpu.get_barrier_semaphore()
    for step in range(1, seq_n):
        pl.semaphore_signal(
            barrier, 1, device_id={"seq": seq_peer(step)}, device_id_type=pl.DeviceIdType.MESH
        )
    for step in range(1, dp_n):
        pl.semaphore_signal(
            barrier, 1, device_id={"dp": dp_peer(step)}, device_id_type=pl.DeviceIdType.MESH
        )
    pl.semaphore_wait(barrier, seq_n + dp_n - 2)
    x_first.wait()

    def enter_row(row, carry):
        load(0, x_hbm.at[row], x_buf).wait()
        act = normed(x_buf[...], gain)
        mixed = dot(inner_ref[...], act) * pick_column(twiddle_t_buf[...], row)
        first_buf[row] = mixed.astype(bf16).reshape(seq_n, cols, channels)
        row_send(first_buf, mixed_hbm, send_sem.at[0], in_sem.at[0], row)
        return carry

    lax.fori_loop(0, rows, enter_row, 0)
    mixed_own = pltpu.make_async_copy(first_buf.at[:, me], mixed_hbm.at[me], own_sem.at[0])
    mixed_own.start()

    for copy in weights:
        copy.wait()

    def grad_row(row, carry):
        loads = [load(0, x_hbm.at[row], x_buf), load(1, cot_hbm.at[row], cot_buf)]
        for copy in loads:
            copy.wait()
        act = normed(x_buf[...], gain)
        for k in range(blocks):
            part = slice(k * size, (k + 1) * size)
            gate_pre, gate_sig = gate_terms(act[:, part], gate_buf[part, :])
            back = dot(cot_buf[:, part], out_buf[part, :], 1, 1)
            grad = (back * gate_pre * gate_sig).astype(bf16)
            second_buf[row, :, :, part] = grad.reshape(seq_n, cols, size)
        row_send(second_buf, scaled_hbm, send_sem.at[1], in_sem.at[1], row)
        return carry

    lax.fori_loop(0, rows, grad_row, 0)
    scaled_own = pltpu.make_async_copy(second_buf.at[:, me], scaled_hbm.at[me], own_sem.at[1])
    scaled_own.start()

    tile = SUB * SUB
    tiles = outer_len // SUB

    def widen_outer(transposed):
        def one(at, carry):
            shape = (tile, outer_len)
            i_of = (lax.broadcasted_iota(jnp.int32, shape, 0) >> 4) + at * SUB
            pick = (i_of == lax.broadcasted_iota(jnp.int32, shape, 1)).astype(bf16)
            picked = dot(pick, outer_ref[...], 1, 1 if transposed else 0).astype(bf16)
            shape = (outer_len, outer_len * SUB)
            p_of = lax.broadcasted_iota(jnp.int32, shape, 1) >> 4
            spread = (p_of == lax.broadcasted_iota(jnp.int32, shape, 0)).astype(bf16)
            full = dot(picked, spread)
            shape = full.shape
            low = lax.broadcasted_iota(jnp.int32, shape, 0) & (SUB - 1)
            high = lax.broadcasted_iota(jnp.int32, shape, 1) & (SUB - 1)
            at_row = pl.multiple_of(at * tile, tile)
            wide_outer[pl.ds(at_row, tile), :] = jnp.where(low == high, full, 0.0).astype(bf16)
            return carry

        lax.fori_loop(0, tiles, one, 0)

    def kernel_column(at, group):
        at_row = pl.multiple_of(at * SUB, SUB)
        table = kernel_buf[pl.ds(at_row, SUB), :]
        spread = jnp.broadcast_to(table[:, None, :], (SUB, SUB, cols)).reshape(tile, cols)
        wanted = (lax.broadcasted_iota(jnp.int32, spread.shape, 0) & (SUB - 1)) + group * SUB
        lanes = lax.broadcasted_iota(jnp.int32, spread.shape, 1)
        return jnp.sum(jnp.where(lanes == wanted, spread, 0.0), axis=-1, keepdims=True)

    tiles_each = rows // SUB

    def mix_outer(source, target, forward):
        def one_block(at, carry):
            group = at // lane_parts
            sub_rows = pl.ds(pl.multiple_of(group * SUB, SUB), SUB)
            lanes = pl.ds(pl.multiple_of((at % lane_parts) * part_cols, part_cols), part_cols)
            load(0, source.at[:, :, sub_rows, lanes], block_buf).wait()

            def whole_of(i):
                return i // tiles_each, pl.ds((i % tiles_each) * SUB, SUB)

            if not forward:

                def scale_tile(i, carry):
                    owner, inside = whole_of(i)
                    held = block_buf[owner, inside].reshape(tile, part_cols).astype(jnp.float32)
                    scaled = (held * kernel_column(i, group)).astype(bf16)
                    block_buf[owner, inside] = scaled.reshape(SUB, SUB, part_cols)
                    return carry

                lax.fori_loop(0, tiles, scale_tile, 0)

            def one_tile(i, carry):
                at_row = pl.multiple_of(i * tile, tile)
                block = block_buf[...].reshape(outer_len * SUB, part_cols)
                mixed = dot(wide_outer[pl.ds(at_row, tile), :], block)
                if forward:
                    mixed = mixed * kernel_column(i, group)
                owner, inside = whole_of(i)
                target[inside, owner, sub_rows, lanes] = mixed.astype(bf16).reshape(
                    SUB, SUB, part_cols
                )
                return carry

            lax.fori_loop(0, tiles, one_tile, 0)
            return carry

        lax.fori_loop(0, cols // SUB * lane_parts, one_block, 0)

    widen_outer(False)
    eye_shape = (inner_len, inner_len)
    eye = lax.broadcasted_iota(jnp.int32, eye_shape, 0) == lax.broadcasted_iota(
        jnp.int32, eye_shape, 1
    )
    inner_t_buf[...] = dot(eye.astype(bf16), inner_ref[...], 1, 1).astype(bf16)

    mixed_own.wait()
    whole(mixed_hbm, send_sem.at[0], in_sem.at[0]).wait()
    mix_outer(mixed_hbm, first_buf, True)

    def seq_send(row, carry):
        row_send(first_buf, seq_hbm, send_sem.at[2], row_sem.at[row], row)
        return carry

    lax.fori_loop(0, rows, seq_send, 0)
    seq_own = pltpu.make_async_copy(first_buf.at[:, me], seq_hbm.at[me], own_sem.at[0])
    seq_own.start()
    widen_outer(True)

    scaled_own.wait()
    whole(scaled_hbm, send_sem.at[1], in_sem.at[1]).wait()
    mix_outer(scaled_hbm, second_buf, False)

    def back_send(row, carry):
        row_send(second_buf, back_hbm, back_send_sem.at[row], back_sem.at[row], row)
        return carry

    ahead = max(rows // 4, 1)
    lax.fori_loop(0, ahead, back_send, 0)
    back_own = pltpu.make_async_copy(second_buf.at[:, me], back_hbm.at[me], own_sem.at[1])
    back_own.start()

    term_buf[...] = jnp.zeros_like(term_buf)
    seq_own.wait()

    def take_row(source, receive, row):
        one_row(source, send_sem.at[2], receive.at[row], row).wait_recv()
        load(3, source.at[:, row], swap_buf).wait()

    def gate_row(row, carry):
        loads = [load(0, x_hbm.at[row], x_buf), load(1, cot_hbm.at[row], cot_buf)]
        take_row(seq_hbm, row_sem, row)
        for copy in loads:
            copy.wait()
        all_act = normed(x_buf[...], gain)
        for k in range(blocks):
            part = slice(k * size, (k + 1) * size)
            act = all_act[:, part]
            cot = cot_buf[:, part]
            gate_pre, gate_sig = gate_terms(act, gate_buf[part, :])
            mix = swap_buf[:, :, part].reshape(inner_len, size).astype(jnp.float32)
            gated = (mix * gate_pre * gate_sig).astype(bf16)
            layer = x_buf[:, part].astype(jnp.float32) + dot(gated, out_buf[part, :])
            result_buf[:, :, part] = layer.astype(bf16).reshape(seq_n, cols, size)
            back = dot(cot, out_buf[part, :], 1, 1)
            grad = (back * mix * gate_sig * (1.0 + gate_pre * (1.0 - gate_sig))).astype(bf16)
            grad_buf[:, part] = grad
            held = term_buf.shape[1:]
            term_buf[k] += dot(act, grad, 0, 0).reshape(held)
            term_buf[blocks + k] += dot(gated, cot, 0, 0).reshape(held)
        stores = [
            store(0, result_buf, layer_hbm.at[row]),
            store(1, grad_buf, grad_hbm.at[row]),
        ]
        for copy in stores:
            copy.wait()
        return carry

    lax.fori_loop(0, rows, gate_row, 0)

    def share_copy(step):
        peer = dp_peer(step)
        return remote(
            term_buf.at[:, peer],
            share_buf.at[my_dp],
            weight_send_sem.at[0, step],
            weight_sem.at[0, step],
            "dp",
            peer,
        )

    def flipped(step):
        index, bit = me, 1
        while bit <= step:
            if step & bit:
                index = index + bit - 2 * bit * (index // bit % 2)
            bit *= 2
        return index

    def piece_copy(bit, step):
        return remote(
            piece_buf.at[step],
            piece_in_buf.at[step],
            weight_send_sem.at[1, step],
            weight_sem.at[1, step],
            "seq",
            flipped(bit),
        )

    bits = [1 << k for k in range(seq_n.bit_length() - 1)]

    def stage_steps(bit):
        return [step for step in range(0, seq_n, bit) if step & bit]

    def send_pieces(bit):
        for step in stage_steps(bit):
            piece_buf[step] = total_buf[step].astype(bf16)
            piece_copy(bit, step).start()

    def add_pieces(bit):
        for step in stage_steps(bit):
            piece_copy(bit, step).wait()
            total_buf[step - bit] += piece_in_buf[step].astype(jnp.float32)

    def final_copy(step):
        peer = dp_peer(step)
        return remote(
            final_buf,
            weight_hbm.at[my_dp],
            weight_send_sem.at[2, step],
            weight_sem.at[2, step],
            "dp",
            peer,
        )

    final_own = pltpu.make_async_copy(final_buf, weight_hbm.at[my_dp], own_sem.at[2])
    for step in range(1, dp_n):
        share_copy(step).start()
    back_own.wait()
    whole(seq_hbm, send_sem.at[2], row_sem.at[0]).wait_send()
    stages = len(bits) + 2
    points = [rows * (k + 1) // (stages + 1) for k in range(stages)]

    def leave_row(row, carry):
        loads = [
            load(0, x_hbm.at[row], x_buf),
            load(1, cot_hbm.at[row], cot_buf),
            load(2, grad_hbm.at[row], grad_buf),
        ]

        @pl.when(row + ahead < rows)
        def _():
            back_send(row + ahead, 0)

        @pl.when(row == points[0])
        def _():
            for step in range(1, dp_n):
                share_copy(step).wait()
            share_buf[my_dp] = term_buf[:, my_dp]
            for step in range(seq_n):
                piece = flipped(step)
                total = share_buf[0, piece]
                for t in range(1, dp_n):
                    total += share_buf[t, piece]
                total_buf[step] = total
            send_pieces(bits[0])

        for stage, bit in enumerate(bits[1:]):

            @pl.when(row == points[stage + 1])
            def _(stage=stage, bit=bit):
                add_pieces(bits[stage])
                send_pieces(bit)

        @pl.when(row == points[len(bits)])
        def _():
            add_pieces(bits[-1])
            final_buf[...] = total_buf[0] * grad_scale
            final_own.start()
            for step in range(1, dp_n):
                final_copy(step).start()

        for copy in loads:
            copy.wait()
        take_row(back_hbm, back_sem, row)
        one_row(back_hbm, back_send_sem.at[row], back_sem.at[row], row).wait_send()
        layer_row = pltpu.make_async_copy(layer_hbm.at[row], second_buf.at[row], layer_sem)
        layer_row.start()
        column = pick_column(twiddle_t_buf[...], row)
        parts = []
        for k in range(blocks):
            part = slice(k * size, (k + 1) * size)
            held = swap_buf[:, :, part].reshape(inner_len, size).astype(jnp.float32)
            twisted = (held * column).astype(bf16)
            parts.append(
                dot(grad_buf[:, part], gate_buf[part, :], 1, 1) + dot(inner_t_buf[...], twisted)
            )
        act_grad = jnp.concatenate(parts, axis=1)
        wide = x_buf[...].astype(jnp.float32)
        scale = row_scale(wide)
        pulled = act_grad * gain
        share = jnp.sum(pulled * wide, axis=-1, keepdims=True) / channels
        grad = pulled * scale - wide * (scale * scale * scale * share)
        result = (cot_buf[...].astype(jnp.float32) + grad).astype(bf16)
        first_buf[row] = result.reshape(seq_n, cols, channels)
        layer_row.wait()
        return carry

    lax.fori_loop(0, rows, leave_row, 0)
    final_own.wait()
    for step in range(1, dp_n):
        final_copy(step).wait()


STORES = 4


def store_kernel(layer_ref, grad_ref, weight_hbm, layer_hbm, input_grad_hbm, weight_out, sem):
    parts = sem.shape[0] // 2
    rows = layer_ref.shape[0] // parts
    copies = [pltpu.make_async_copy(weight_hbm, weight_out, sem.at[2 * parts])]
    for k in range(parts):
        part = pl.ds(k * rows, rows)
        copies.append(
            pltpu.make_async_copy(layer_ref.at[part], layer_hbm.at[part], sem.at[2 * k])
        )
        copies.append(
            pltpu.make_async_copy(grad_ref.at[part], input_grad_hbm.at[part], sem.at[2 * k + 1])
        )
    for copy in copies:
        copy.start()
    for copy in copies:
        copy.wait()


def shards_fast(
    inputs,
    norm_gain,
    inner_mix,
    twiddle,
    outer_mix,
    long_kernel,
    gate_weight,
    out_weight,
    cotangent,
):
    _, rows_local, channels = inputs.shape
    inner_len = inner_mix.shape[0]
    outer_len = outer_mix.shape[0]
    rows = rows_local // inner_len
    size = gate_weight.shape[1]
    blocks = gate_weight.shape[0] // size
    seq_n = lax.axis_size("seq")
    dp_n = lax.axis_size("dp")
    cols = inner_len // seq_n
    piece = size // dp_n
    grad_scale = 1.0 / math.sqrt(dp_n * rows_local * seq_n)
    bf16 = jnp.bfloat16
    f32 = jnp.float32
    part_cols = channels // 2

    row_shape = jax.ShapeDtypeStruct((rows, inner_len, channels), bf16)
    swap_shape = jax.ShapeDtypeStruct((seq_n, rows, cols, channels), bf16)
    held = pl.BlockSpec(memory_space=pltpu.VMEM)
    anywhere = pl.BlockSpec(memory_space=pl.ANY)
    row_buf = pltpu.VMEM((inner_len, channels), bf16)
    sems = pltpu.SemaphoreType.DMA

    input_grad, layer_out, weight_grads = pl.pallas_call(
        functools.partial(layer_kernel, grad_scale),
        in_specs=[held] * 5 + [anywhere] * 4,
        out_specs=[held] * 2 + [anywhere] * 7,
        out_shape=[
            pltpu.VMEM((rows, seq_n, cols, channels), bf16),
            pltpu.VMEM((rows, seq_n, cols, channels), bf16),
            jax.ShapeDtypeStruct((dp_n, piece, size), f32),
            jax.ShapeDtypeStruct((rows, seq_n, cols, channels), bf16),
            row_shape,
        ]
        + [swap_shape] * 4,
        scratch_shapes=[
            pltpu.VMEM((inner_len, rows), f32),
            pltpu.VMEM((outer_len, cols), f32),
            pltpu.VMEM((blocks * size, size), bf16),
            pltpu.VMEM((blocks * size, size), bf16),
            pltpu.VMEM((outer_len * SUB, outer_len * SUB), bf16),
            pltpu.VMEM((seq_n, rows, SUB, part_cols), bf16),
            row_buf,
            row_buf,
            row_buf,
            pltpu.VMEM((seq_n, cols, channels), bf16),
            pltpu.VMEM((seq_n, cols, channels), bf16),
            pltpu.VMEM((inner_len, inner_len), bf16),
            pltpu.VMEM((seq_n, dp_n, piece, size), f32),
            pltpu.VMEM((dp_n, seq_n, piece, size), f32),
            pltpu.VMEM((seq_n, piece, size), f32),
            pltpu.VMEM((seq_n, piece, size), bf16),
            pltpu.VMEM((seq_n, piece, size), bf16),
            pltpu.VMEM((piece, size), f32),
            sems((4,)),
            sems((2,)),
            sems((3,)),
            sems((3,)),
            sems((2,)),
            sems((rows,)),
            sems((rows,)),
            sems((rows,)),
            sems,
            sems((3, max(seq_n, dp_n))),
            sems((3, max(seq_n, dp_n))),
        ],
        compiler_params=pltpu.CompilerParams(
            collective_id=0, has_side_effects=True, vmem_limit_bytes=30 * 2**20
        ),
        cost_estimate=pl.CostEstimate(
            flops=24 * rows_local * channels * size,
            bytes_accessed=40 * rows_local * channels,
            transcendentals=0,
        ),
        name="layer",
    )(
        norm_gain,
        inner_mix,
        twiddle,
        outer_mix,
        long_kernel.T,
        gate_weight,
        out_weight,
        inputs.reshape(row_shape.shape),
        cotangent.reshape(row_shape.shape),
    )[:3]
    layer_out, input_grad, weight_grads = pl.pallas_call(
        store_kernel,
        in_specs=[held] * 2 + [pl.BlockSpec(memory_space=pltpu.HBM)],
        out_specs=[anywhere] * 3,
        out_shape=[jax.ShapeDtypeStruct(a.shape, a.dtype) for a in (layer_out, input_grad, weight_grads)],
        scratch_shapes=[sems((2 * STORES + 1,))],
        compiler_params=pltpu.CompilerParams(vmem_limit_bytes=2**20),
        name="store",
    )(layer_out, input_grad, weight_grads)
    return (
        layer_out.reshape(inputs.shape),
        input_grad.reshape(inputs.shape),
        weight_grads.reshape(dp_n * piece, size),
    )


def shards(*arrays):
    batch, rows_local, channels = arrays[0].shape
    inner_len = arrays[2].shape[0]
    cols = arrays[5].shape[1]
    size = arrays[6].shape[1]
    blocks = arrays[6].shape[0] // size
    seq_n, dp_n = lax.axis_size("seq"), lax.axis_size("dp")
    fits = (
        batch == 1
        and min(seq_n, dp_n) > 1
        and seq_n & (seq_n - 1) == 0
        and rows_local // inner_len % SUB == 0
        and cols % SUB == 0
        and channels % 256 == 0
        and size % 128 == 0
        and 2 * blocks == seq_n
        and size % (16 * dp_n) == 0
        and inner_len % 128 == 0
    )
    if fits:
        return shards_fast(*arrays)
    return shards_plain(*arrays)


def solution(mesh):
    return jax.shard_map(
        shards,
        mesh=mesh,
        in_specs=(
            P(("groups", "dp"), "seq", None),
            P(),
            P(),
            P("seq", None),
            P(),
            P(None, "seq"),
            P(),
            P(),
            P(("groups", "dp"), "seq", None),
        ),
        out_specs=(
            P(("groups", "dp"), "seq", None),
            P(("groups", "dp"), "seq", None),
            P(("groups", "seq"), None),
        ),
        check_vma=False,
    )
```

```python
import functools
import math

import jax
import jax.numpy as jnp
from jax import lax
from jax.experimental import pallas as pl
from jax.experimental.pallas import tpu as pltpu
from jax.sharding import PartitionSpec as P

norm_eps = 1e-06


def normalize(values, norm_gain):
    mean_square = jnp.mean(values * values, axis=-1, keepdims=True)
    return values * lax.rsqrt(mean_square + norm_eps) * norm_gain


def block_apply(operand, weight):
    blocks = weight.shape[0] // weight.shape[1]
    grouped = operand.reshape(operand.shape[0], blocks, weight.shape[1])
    stacked = weight.reshape(blocks, weight.shape[1], weight.shape[1])
    result = jnp.einsum("rki,kij->rkj", grouped, stacked, preferred_element_type=jnp.float32)
    return result.reshape(operand.shape[0], -1)


def block_back(partner, weight):
    blocks = weight.shape[0] // weight.shape[1]
    grouped = partner.reshape(partner.shape[0], blocks, weight.shape[1])
    stacked = weight.reshape(blocks, weight.shape[1], weight.shape[1])
    result = jnp.einsum("rkj,kij->rki", grouped, stacked, preferred_element_type=jnp.float32)
    return result.reshape(partner.shape[0], -1)


def block_term(operand, partner, blocks, block_size):
    grouped = operand.reshape(operand.shape[0], blocks, block_size)
    other_rows = partner.reshape(partner.shape[0], blocks, block_size)
    result = jnp.einsum("rki,rkj->kij", grouped, other_rows, preferred_element_type=jnp.float32)
    return result.reshape(blocks * block_size, block_size)


def to_columns(row_layout):
    return lax.all_to_all(row_layout, "seq", split_axis=2, concat_axis=1, tiled=True)


def to_rows(col_layout):
    return lax.all_to_all(col_layout, "seq", split_axis=1, concat_axis=2, tiled=True)


def shards_plain(
    inputs,
    norm_gain,
    inner_mix,
    twiddle,
    outer_mix,
    long_kernel,
    gate_weight,
    out_weight,
    cotangent,
):
    batch_local, rows_local, channels = inputs.shape
    inner_len = inner_mix.shape[0]
    local_outer = rows_local // inner_len
    flat_rows = batch_local * rows_local
    block_size = gate_weight.shape[1]
    blocks = gate_weight.shape[0] // block_size
    all_tokens = batch_local * lax.axis_size("dp") * rows_local * lax.axis_size("seq")
    grad_scale = 1.0 / math.sqrt(all_tokens)
    inputs_wide = inputs.reshape(flat_rows, channels).astype(jnp.float32)
    activation = normalize(inputs_wide, norm_gain).astype(jnp.bfloat16)
    grid_rows = activation.reshape(batch_local, local_outer, inner_len, channels)
    inner_out = jnp.einsum(
        "jq,bpqd->bpjd", inner_mix, grid_rows, preferred_element_type=jnp.float32
    )
    mixed_rows = (inner_out * twiddle[None, :, :, None]).astype(jnp.bfloat16)
    columns = to_columns(mixed_rows)
    outer_out = jnp.einsum("ip,bpjd->bijd", outer_mix, columns, preferred_element_type=jnp.float32)
    mixed_cols = (outer_out * long_kernel[None, :, :, None]).astype(jnp.bfloat16)
    seq_mix = to_rows(mixed_cols).reshape(flat_rows, channels)
    gate_pre = block_apply(activation, gate_weight)
    gate_sig = jax.nn.sigmoid(gate_pre)
    mix_wide = seq_mix.astype(jnp.float32)
    gated_rows = (mix_wide * gate_pre * gate_sig).astype(jnp.bfloat16)
    layer_out = (inputs_wide + block_apply(gated_rows, out_weight)).astype(jnp.bfloat16)
    cotan_rows = cotangent.reshape(flat_rows, channels)
    back_gated = block_back(cotan_rows, out_weight)
    mix_grad = (back_gated * gate_pre * gate_sig).astype(jnp.bfloat16)
    gate_grad = (back_gated * mix_wide * gate_sig * (1.0 + gate_pre * (1.0 - gate_sig))).astype(
        jnp.bfloat16
    )
    act_grad = block_back(gate_grad, gate_weight)
    weight_term = jnp.concatenate(
        [
            block_term(activation, gate_grad, blocks, block_size),
            block_term(gated_rows, cotan_rows, blocks, block_size),
        ],
        axis=0,
    )
    grad_cols = to_columns(mix_grad.reshape(batch_local, local_outer, inner_len, channels))
    scaled_back = (grad_cols.astype(jnp.float32) * long_kernel[None, :, :, None]).astype(
        jnp.bfloat16
    )
    back_outer = jnp.einsum(
        "ip,bijd->bpjd", outer_mix, scaled_back, preferred_element_type=jnp.float32
    ).astype(jnp.bfloat16)
    back_rows = to_rows(back_outer)
    twisted = (back_rows.astype(jnp.float32) * twiddle[None, :, :, None]).astype(jnp.bfloat16)
    inner_back = jnp.einsum("jq,bpjd->bpqd", inner_mix, twisted, preferred_element_type=jnp.float32)
    act_grad = act_grad + inner_back.reshape(flat_rows, channels)
    pullback = jax.vjp(lambda wide_rows: normalize(wide_rows, norm_gain), inputs_wide)[1]
    input_grad = (cotan_rows.astype(jnp.float32) + pullback(act_grad)[0]).astype(jnp.bfloat16)
    shard_term = lax.psum_scatter(weight_term, "seq", scatter_dimension=0, tiled=True)
    weight_grads = lax.psum(shard_term, "dp") * grad_scale
    return (layer_out.reshape(inputs.shape), input_grad.reshape(inputs.shape), weight_grads)


def dot(lhs, rhs, lhs_dim=1, rhs_dim=0):
    return lax.dot_general(
        lhs, rhs, (((lhs_dim,), (rhs_dim,)), ((), ())), preferred_element_type=jnp.float32
    )


def row_scale(wide):
    return lax.rsqrt(jnp.sum(wide * wide, axis=-1, keepdims=True) / wide.shape[-1] + norm_eps)


def pick_column(table, at):
    lanes = lax.broadcasted_iota(jnp.int32, table.shape, 1)
    return jnp.sum(jnp.where(lanes == at, table, 0.0), axis=-1, keepdims=True)


def normed(rows, gain):
    wide = rows.astype(jnp.float32)
    return (wide * row_scale(wide) * gain).astype(jnp.bfloat16)


def gate_terms(act, weight):
    gate_pre = dot(act, weight)
    gate_sig = jax.nn.sigmoid(gate_pre)
    return gate_pre, gate_sig


SUB = 16


def leave(x_ref, cot_ref, grad_ref, back_ref, row, twiddle_t_ref, inner_t_ref, gate_ref, gain):
    size = gate_ref.shape[1]
    inner_len, channels = x_ref.shape
    column = pick_column(twiddle_t_ref[...], row)
    parts = []
    for k in range(channels // size):
        part = slice(k * size, (k + 1) * size)
        held = back_ref[:, :, part].reshape(inner_len, size).astype(jnp.float32)
        twisted = (held * column).astype(jnp.bfloat16)
        parts.append(
            dot(grad_ref[:, part], gate_ref[part, :], 1, 1) + dot(inner_t_ref[...], twisted)
        )
    act_grad = jnp.concatenate(parts, axis=1)
    wide = x_ref[...].astype(jnp.float32)
    scale = row_scale(wide)
    pulled = act_grad * gain
    share = jnp.sum(pulled * wide, axis=-1, keepdims=True) / channels
    grad = pulled * scale - wide * (scale * scale * scale * share)
    return (cot_ref[...].astype(jnp.float32) + grad).astype(jnp.bfloat16)


def layer_kernel(
    grad_scale,
    gain_ref,
    inner_ref,
    twiddle_ref,
    outer_ref,
    kernel_ref,
    gate_hbm,
    out_hbm,
    x_hbm,
    cot_hbm,
    weight_buf,
    x_buf,
    cot_buf,
    grad_buf,
    last_buf,
    result_buf,
    gate_buf,
    inner_t_buf,
    twiddle_t_buf,
    gain_buf,
    first_buf,
    second_buf,
    layer_hbm,
    grad_hbm,
    mixed_hbm,
    scaled_hbm,
    seq_hbm,
    back_hbm,
    kernel_buf,
    out_buf,
    wide_outer,
    block_buf,
    swap_buf,
    term_buf,
    share_buf,
    total_buf,
    piece_buf,
    piece_in_buf,
    final_buf,
    load_sem,
    store_sem,
    own_sem,
    send_sem,
    in_sem,
    row_sem,
    back_sem,
    back_send_sem,
    layer_sem,
    weight_send_sem,
    weight_sem,
):
    rows, seq_n, cols, channels = first_buf.shape
    dp_n = share_buf.shape[0]
    outer_len = seq_n * rows
    inner_len = seq_n * cols
    size = gate_buf.shape[1]
    blocks = channels // size
    part_cols = block_buf.shape[-1]
    lane_parts = channels // part_cols
    me = lax.axis_index("seq")
    my_dp = lax.axis_index("dp")
    gain = gain_ref[...].reshape(1, channels)
    last = rows - 1
    bf16 = jnp.bfloat16

    def seq_peer(step):
        return lax.rem(me + step, seq_n)

    def dp_peer(step):
        return lax.rem(my_dp + step, dp_n)

    def remote(source, target, send, receive, axis, index):
        return pltpu.make_async_remote_copy(
            src_ref=source,
            dst_ref=target,
            send_sem=send,
            recv_sem=receive,
            device_id={axis: index},
            device_id_type=pl.DeviceIdType.MESH,
        )

    def load(sem, source, target):
        copy = pltpu.make_async_copy(source, target, load_sem.at[sem])
        copy.start()
        return copy

    def store(sem, source, target):
        copy = pltpu.make_async_copy(source, target, store_sem.at[sem])
        copy.start()
        return copy

    def row_send(buf, target, send, receive, row):
        for step in range(1, seq_n):
            peer = seq_peer(step)
            remote(buf.at[row, peer], target.at[me, row], send, receive, "seq", peer).start()

    others = pl.ds(0, seq_n - 1)

    def whole(target, send, receive):
        return remote(target.at[others], target.at[others], send, receive, "seq", seq_peer(1))

    def one_row(target, send, receive, row):
        held = target.at[others, row]
        return remote(held, held, send, receive, "seq", seq_peer(1))

    x_first = load(0, x_hbm.at[0], x_buf)
    weights = [load(2, gate_hbm, gate_buf), load(3, out_hbm, out_buf)]
    twiddle_t_buf[...] = twiddle_ref[...].T
    kernel_buf[...] = kernel_ref[...].T
    gain_buf[...] = gain
    barrier = pltpu.get_barrier_semaphore()
    for step in range(1, seq_n):
        pl.semaphore_signal(
            barrier, 1, device_id={"seq": seq_peer(step)}, device_id_type=pl.DeviceIdType.MESH
        )
    for step in range(1, dp_n):
        pl.semaphore_signal(
            barrier, 1, device_id={"dp": dp_peer(step)}, device_id_type=pl.DeviceIdType.MESH
        )
    pl.semaphore_wait(barrier, seq_n + dp_n - 2)
    x_first.wait()

    def enter_row(row, carry):
        load(0, x_hbm.at[row], x_buf).wait()
        act = normed(x_buf[...], gain)
        for step in list(range(1, seq_n)) + [0]:
            peer = seq_peer(step)
            owned = pl.ds(pl.multiple_of(peer * cols, cols), cols)
            mixed = dot(inner_ref[owned, :], act) * pick_column(twiddle_t_buf[owned, :], row)
            first_buf[row, peer] = mixed.astype(bf16)
            if step:
                remote(
                    first_buf.at[row, peer],
                    mixed_hbm.at[me, row],
                    send_sem.at[0],
                    in_sem.at[0],
                    "seq",
                    peer,
                ).start()
        return carry

    lax.fori_loop(0, rows, enter_row, 0)
    mixed_own = pltpu.make_async_copy(first_buf.at[:, me], mixed_hbm.at[me], own_sem.at[0])
    mixed_own.start()

    for copy in weights:
        copy.wait()

    def grad_row(row, carry):
        loads = [load(0, x_hbm.at[row], x_buf), load(1, cot_hbm.at[row], cot_buf)]
        for copy in loads:
            copy.wait()
        act = normed(x_buf[...], gain)
        for k in range(blocks):
            part = slice(k * size, (k + 1) * size)
            gate_pre, gate_sig = gate_terms(act[:, part], gate_buf[part, :])
            back = dot(cot_buf[:, part], out_buf[part, :], 1, 1)
            grad = (back * gate_pre * gate_sig).astype(bf16)
            second_buf[row, :, :, part] = grad.reshape(seq_n, cols, size)
        row_send(second_buf, scaled_hbm, send_sem.at[1], in_sem.at[1], row)
        return carry

    lax.fori_loop(0, rows, grad_row, 0)
    scaled_own = pltpu.make_async_copy(second_buf.at[:, me], scaled_hbm.at[me], own_sem.at[1])
    scaled_own.start()

    tile = SUB * SUB
    tiles = outer_len // SUB

    def widen_outer(transposed):
        def one(at, carry):
            shape = (tile, outer_len)
            i_of = (lax.broadcasted_iota(jnp.int32, shape, 0) >> 4) + at * SUB
            pick = (i_of == lax.broadcasted_iota(jnp.int32, shape, 1)).astype(bf16)
            picked = dot(pick, outer_ref[...], 1, 1 if transposed else 0).astype(bf16)
            shape = (outer_len, outer_len * SUB)
            p_of = lax.broadcasted_iota(jnp.int32, shape, 1) >> 4
            spread = (p_of == lax.broadcasted_iota(jnp.int32, shape, 0)).astype(bf16)
            full = dot(picked, spread)
            shape = full.shape
            low = lax.broadcasted_iota(jnp.int32, shape, 0) & (SUB - 1)
            high = lax.broadcasted_iota(jnp.int32, shape, 1) & (SUB - 1)
            at_row = pl.multiple_of(at * tile, tile)
            wide_outer[pl.ds(at_row, tile), :] = jnp.where(low == high, full, 0.0).astype(bf16)
            return carry

        lax.fori_loop(0, tiles, one, 0)

    def kernel_column(at, group):
        at_row = pl.multiple_of(at * SUB, SUB)
        table = kernel_buf[pl.ds(at_row, SUB), :]
        spread = jnp.broadcast_to(table[:, None, :], (SUB, SUB, cols)).reshape(tile, cols)
        wanted = (lax.broadcasted_iota(jnp.int32, spread.shape, 0) & (SUB - 1)) + group * SUB
        lanes = lax.broadcasted_iota(jnp.int32, spread.shape, 1)
        return jnp.sum(jnp.where(lanes == wanted, spread, 0.0), axis=-1, keepdims=True)

    tiles_each = rows // SUB

    def mix_outer(source, target, forward):
        def one_block(at, carry):
            group = at // lane_parts
            sub_rows = pl.ds(pl.multiple_of(group * SUB, SUB), SUB)
            lanes = pl.ds(pl.multiple_of((at % lane_parts) * part_cols, part_cols), part_cols)
            load(0, source.at[:, :, sub_rows, lanes], block_buf).wait()

            def whole_of(i):
                return i // tiles_each, pl.ds((i % tiles_each) * SUB, SUB)

            if not forward:

                def scale_tile(i, carry):
                    owner, inside = whole_of(i)
                    held = block_buf[owner, inside].reshape(tile, part_cols).astype(jnp.float32)
                    scaled = (held * kernel_column(i, group)).astype(bf16)
                    block_buf[owner, inside] = scaled.reshape(SUB, SUB, part_cols)
                    return carry

                lax.fori_loop(0, tiles, scale_tile, 0)

            def one_tile(i, carry):
                at_row = pl.multiple_of(i * tile, tile)
                block = block_buf[...].reshape(outer_len * SUB, part_cols)
                mixed = dot(wide_outer[pl.ds(at_row, tile), :], block)
                if forward:
                    mixed = mixed * kernel_column(i, group)
                owner, inside = whole_of(i)
                target[inside, owner, sub_rows, lanes] = mixed.astype(bf16).reshape(
                    SUB, SUB, part_cols
                )
                return carry

            lax.fori_loop(0, tiles, one_tile, 0)
            return carry

        lax.fori_loop(0, cols // SUB * lane_parts, one_block, 0)

    widen_outer(False)
    eye_shape = (inner_len, inner_len)
    eye = lax.broadcasted_iota(jnp.int32, eye_shape, 0) == lax.broadcasted_iota(
        jnp.int32, eye_shape, 1
    )
    inner_t_buf[...] = dot(eye.astype(bf16), inner_ref[...], 1, 1).astype(bf16)

    mixed_own.wait()
    whole(mixed_hbm, send_sem.at[0], in_sem.at[0]).wait()
    mix_outer(mixed_hbm, first_buf, True)

    def seq_send(row, carry):
        row_send(first_buf, seq_hbm, send_sem.at[2], row_sem.at[row], row)
        return carry

    lax.fori_loop(0, rows, seq_send, 0)
    seq_own = pltpu.make_async_copy(first_buf.at[:, me], seq_hbm.at[me], own_sem.at[0])
    seq_own.start()
    widen_outer(True)

    scaled_own.wait()
    whole(scaled_hbm, send_sem.at[1], in_sem.at[1]).wait()
    mix_outer(scaled_hbm, second_buf, False)

    def back_send(row, carry):
        @pl.when(row < last)
        def _():
            row_send(second_buf, back_hbm, back_send_sem.at[row], back_sem.at[row], row)

        @pl.when(row == last)
        def _():
            for step in range(1, seq_n):
                peer = seq_peer(step)
                remote(
                    second_buf.at[row, peer],
                    last_buf.at[me],
                    back_send_sem.at[row],
                    back_sem.at[row],
                    "seq",
                    peer,
                ).start()

        return carry

    last_buf[me] = second_buf[last, me]

    ahead = max(rows // 4, 1)
    lax.fori_loop(0, ahead, back_send, 0)
    back_own = pltpu.make_async_copy(second_buf.at[:, me], back_hbm.at[me], own_sem.at[1])
    back_own.start()

    term_buf[...] = jnp.zeros_like(term_buf)
    seq_own.wait()

    def take_row(source, receive, row):
        one_row(source, send_sem.at[2], receive.at[row], row).wait_recv()
        load(3, source.at[:, row], swap_buf).wait()

    def gate_row(row, carry):
        loads = [load(0, x_hbm.at[row], x_buf), load(1, cot_hbm.at[row], cot_buf)]
        take_row(seq_hbm, row_sem, row)
        for copy in loads:
            copy.wait()
        all_act = normed(x_buf[...], gain)
        for k in range(blocks):
            part = slice(k * size, (k + 1) * size)
            act = all_act[:, part]
            cot = cot_buf[:, part]
            gate_pre, gate_sig = gate_terms(act, gate_buf[part, :])
            mix = swap_buf[:, :, part].reshape(inner_len, size).astype(jnp.float32)
            gated = (mix * gate_pre * gate_sig).astype(bf16)
            layer = x_buf[:, part].astype(jnp.float32) + dot(gated, out_buf[part, :])
            result_buf[:, :, part] = layer.astype(bf16).reshape(seq_n, cols, size)
            back = dot(cot, out_buf[part, :], 1, 1)
            grad = (back * mix * gate_sig * (1.0 + gate_pre * (1.0 - gate_sig))).astype(bf16)
            grad_buf[:, part] = grad
            held = term_buf.shape[1:]
            term_buf[k] += dot(act, grad, 0, 0).reshape(held)
            term_buf[blocks + k] += dot(gated, cot, 0, 0).reshape(held)
        stores = [
            store(0, result_buf, layer_hbm.at[row]),
            store(1, grad_buf, grad_hbm.at[row]),
        ]
        for copy in stores:
            copy.wait()
        return carry

    lax.fori_loop(0, rows, gate_row, 0)

    def share_copy(step):
        peer = dp_peer(step)
        return remote(
            term_buf.at[:, peer],
            share_buf.at[my_dp],
            weight_send_sem.at[0, step],
            weight_sem.at[0, step],
            "dp",
            peer,
        )

    def flipped(step):
        index, bit = me, 1
        while bit <= step:
            if step & bit:
                index = index + bit - 2 * bit * (index // bit % 2)
            bit *= 2
        return index

    def piece_copy(bit, step):
        return remote(
            piece_buf.at[step],
            piece_in_buf.at[step],
            weight_send_sem.at[1, step],
            weight_sem.at[1, step],
            "seq",
            flipped(bit),
        )

    bits = [1 << k for k in range(seq_n.bit_length() - 1)]

    def stage_steps(bit):
        return [step for step in range(0, seq_n, bit) if step & bit]

    def send_pieces(bit):
        for step in stage_steps(bit):
            piece_buf[step] = total_buf[step].astype(bf16)
            piece_copy(bit, step).start()

    def add_pieces(bit):
        for step in stage_steps(bit):
            piece_copy(bit, step).wait()
            total_buf[step - bit] += piece_in_buf[step].astype(jnp.float32)

    def final_copy(step):
        peer = dp_peer(step)
        return remote(
            final_buf,
            weight_buf.at[my_dp],
            weight_send_sem.at[2, step],
            weight_sem.at[2, step],
            "dp",
            peer,
        )

    for step in range(1, dp_n):
        share_copy(step).start()
    back_own.wait()
    whole(seq_hbm, send_sem.at[2], row_sem.at[0]).wait_send()
    stages = len(bits) + 2
    points = [rows * (k + 1) // (stages + 1) for k in range(stages)]

    def leave_row(row, carry):
        loads = [
            load(0, x_hbm.at[row], x_buf),
            load(1, cot_hbm.at[row], cot_buf),
            load(2, grad_hbm.at[row], grad_buf),
        ]

        @pl.when(row + ahead < rows)
        def _():
            back_send(row + ahead, 0)

        @pl.when(row == points[0])
        def _():
            for step in range(1, dp_n):
                share_copy(step).wait()
            share_buf[my_dp] = term_buf[:, my_dp]
            for step in range(seq_n):
                piece = flipped(step)
                total = share_buf[0, piece]
                for t in range(1, dp_n):
                    total += share_buf[t, piece]
                total_buf[step] = total
            send_pieces(bits[0])

        for stage, bit in enumerate(bits[1:]):

            @pl.when(row == points[stage + 1])
            def _(stage=stage, bit=bit):
                add_pieces(bits[stage])
                send_pieces(bit)

        @pl.when(row == points[len(bits)])
        def _():
            add_pieces(bits[-1])
            final_buf[...] = total_buf[0] * grad_scale
            weight_buf[my_dp] = final_buf[...]
            for step in range(1, dp_n):
                final_copy(step).start()

        for copy in loads:
            copy.wait()
        take_row(back_hbm, back_sem, row)
        one_row(back_hbm, back_send_sem.at[row], back_sem.at[row], row).wait_send()
        layer_row = pltpu.make_async_copy(layer_hbm.at[row], second_buf.at[row], layer_sem)
        layer_row.start()
        result = leave(
            x_buf, cot_buf, grad_buf, swap_buf, row, twiddle_t_buf, inner_t_buf, gate_buf, gain
        )
        first_buf[row] = result.reshape(seq_n, cols, channels)
        layer_row.wait()
        return carry

    lax.fori_loop(0, last, leave_row, 0)
    loads = [
        load(0, x_hbm.at[last], x_buf),
        load(1, cot_hbm.at[last], cot_buf),
        load(2, grad_hbm.at[last], grad_buf),
    ]
    for copy in loads:
        copy.wait()
    for step in range(1, dp_n):
        final_copy(step).wait()
    landed = last_buf.at[others]
    remote(landed, landed, back_send_sem.at[last], back_sem.at[last], "seq", seq_peer(1)).wait()


STORES = 2


def store_kernel(
    weight_ref,
    x_ref,
    cot_ref,
    mid_ref,
    back_ref,
    last_layer_ref,
    gate_ref,
    inner_t_ref,
    twiddle_t_ref,
    gain_ref,
    grad_ref,
    layer_ref,
    layer_hbm,
    input_grad_hbm,
    weight_hbm,
    last_grad_ref,
    sem,
):
    last = grad_ref.shape[0] - 1
    copies = []

    def store(source, target):
        copy = pltpu.make_async_copy(source, target, sem.at[len(copies)])
        copies.append(copy)
        copy.start()

    for k in range(STORES):
        part = pl.ds(k * last // STORES, (k + 1) * last // STORES - k * last // STORES)
        store(layer_ref.at[part], layer_hbm.at[part])
        store(grad_ref.at[part], input_grad_hbm.at[part])
    store(last_layer_ref, layer_hbm.at[last])
    store(weight_ref, weight_hbm)
    result = leave(
        x_ref,
        cot_ref,
        mid_ref,
        back_ref,
        last,
        twiddle_t_ref,
        inner_t_ref,
        gate_ref,
        gain_ref[...],
    )
    last_grad_ref[...] = result.reshape(last_grad_ref.shape)
    store(last_grad_ref, input_grad_hbm.at[last])
    for copy in copies:
        copy.wait()


def shards_fast(
    inputs,
    norm_gain,
    inner_mix,
    twiddle,
    outer_mix,
    long_kernel,
    gate_weight,
    out_weight,
    cotangent,
):
    _, rows_local, channels = inputs.shape
    inner_len = inner_mix.shape[0]
    outer_len = outer_mix.shape[0]
    rows = rows_local // inner_len
    size = gate_weight.shape[1]
    blocks = gate_weight.shape[0] // size
    seq_n = lax.axis_size("seq")
    dp_n = lax.axis_size("dp")
    cols = inner_len // seq_n
    piece = size // dp_n
    grad_scale = 1.0 / math.sqrt(dp_n * rows_local * seq_n)
    bf16 = jnp.bfloat16
    f32 = jnp.float32
    part_cols = channels // 2

    row_shape = jax.ShapeDtypeStruct((rows, inner_len, channels), bf16)
    swap_shape = jax.ShapeDtypeStruct((seq_n, rows, cols, channels), bf16)
    held = pl.BlockSpec(memory_space=pltpu.VMEM)
    anywhere = pl.BlockSpec(memory_space=pl.ANY)
    row_buf = pltpu.VMEM((inner_len, channels), bf16)
    sems = pltpu.SemaphoreType.DMA

    grid_shape = (rows, seq_n, cols, channels)
    piece_row = (seq_n, cols, channels)
    kept = pl.pallas_call(
        functools.partial(layer_kernel, grad_scale),
        in_specs=[held] * 5 + [anywhere] * 4,
        out_specs=[held] * 12 + [anywhere] * 6,
        out_shape=[
            pltpu.VMEM((dp_n, piece, size), f32),
            row_buf,
            row_buf,
            row_buf,
            pltpu.VMEM(piece_row, bf16),
            pltpu.VMEM(piece_row, bf16),
            pltpu.VMEM((blocks * size, size), bf16),
            pltpu.VMEM((inner_len, inner_len), bf16),
            pltpu.VMEM((inner_len, rows), f32),
            pltpu.VMEM((1, channels), f32),
            pltpu.VMEM(grid_shape, bf16),
            pltpu.VMEM(grid_shape, bf16),
            jax.ShapeDtypeStruct(grid_shape, bf16),
            row_shape,
        ]
        + [swap_shape] * 4,
        scratch_shapes=[
            pltpu.VMEM((outer_len, cols), f32),
            pltpu.VMEM((blocks * size, size), bf16),
            pltpu.VMEM((outer_len * SUB, outer_len * SUB), bf16),
            pltpu.VMEM((seq_n, rows, SUB, part_cols), bf16),
            pltpu.VMEM(piece_row, bf16),
            pltpu.VMEM((seq_n, dp_n, piece, size), f32),
            pltpu.VMEM((dp_n, seq_n, piece, size), f32),
            pltpu.VMEM((seq_n, piece, size), f32),
            pltpu.VMEM((seq_n, piece, size), bf16),
            pltpu.VMEM((seq_n, piece, size), bf16),
            pltpu.VMEM((piece, size), f32),
            sems((4,)),
            sems((2,)),
            sems((3,)),
            sems((3,)),
            sems((2,)),
            sems((rows,)),
            sems((rows,)),
            sems((rows,)),
            sems,
            sems((3, max(seq_n, dp_n))),
            sems((3, max(seq_n, dp_n))),
        ],
        compiler_params=pltpu.CompilerParams(
            collective_id=0, has_side_effects=True, vmem_limit_bytes=30 * 2**20
        ),
        cost_estimate=pl.CostEstimate(
            flops=24 * rows_local * channels * size,
            bytes_accessed=40 * rows_local * channels,
            transcendentals=0,
        ),
        name="layer",
    )(
        norm_gain,
        inner_mix,
        twiddle,
        outer_mix,
        long_kernel.T,
        gate_weight,
        out_weight,
        inputs.reshape(row_shape.shape),
        cotangent.reshape(row_shape.shape),
    )[:12]
    layer_out, input_grad, weight_grads = pl.pallas_call(
        store_kernel,
        in_specs=[held] * len(kept),
        out_specs=[anywhere] * 3,
        out_shape=[jax.ShapeDtypeStruct(a.shape, a.dtype) for a in (kept[-1], kept[-2], kept[0])],
        scratch_shapes=[pltpu.VMEM(piece_row, bf16), sems((2 * STORES + 3,))],
        compiler_params=pltpu.CompilerParams(vmem_limit_bytes=5 * 2**20),
        name="store",
    )(*kept)
    return (
        layer_out.reshape(inputs.shape),
        input_grad.reshape(inputs.shape),
        weight_grads.reshape(dp_n * piece, size),
    )


def shards(*arrays):
    batch, rows_local, channels = arrays[0].shape
    inner_len = arrays[2].shape[0]
    cols = arrays[5].shape[1]
    size = arrays[6].shape[1]
    blocks = arrays[6].shape[0] // size
    seq_n, dp_n = lax.axis_size("seq"), lax.axis_size("dp")
    fits = (
        batch == 1
        and min(seq_n, dp_n) > 1
        and seq_n & (seq_n - 1) == 0
        and rows_local // inner_len % SUB == 0
        and cols % SUB == 0
        and channels % 256 == 0
        and size % 128 == 0
        and 2 * blocks == seq_n
        and size % (16 * dp_n) == 0
        and inner_len % 128 == 0
    )
    if fits:
        return shards_fast(*arrays)
    return shards_plain(*arrays)


def solution(mesh):
    return jax.shard_map(
        shards,
        mesh=mesh,
        in_specs=(
            P(("groups", "dp"), "seq", None),
            P(),
            P(),
            P("seq", None),
            P(),
            P(None, "seq"),
            P(),
            P(),
            P(("groups", "dp"), "seq", None),
        ),
        out_specs=(
            P(("groups", "dp"), "seq", None),
            P(("groups", "dp"), "seq", None),
            P(("groups", "seq"), None),
        ),
        check_vma=False,
    )
```

```python
import functools
import math

import jax
import jax.numpy as jnp
from jax import lax
from jax.experimental import pallas as pl
from jax.experimental.pallas import tpu as pltpu
from jax.sharding import PartitionSpec as P

norm_eps = 1e-06


def normalize(values, norm_gain):
    mean_square = jnp.mean(values * values, axis=-1, keepdims=True)
    return values * lax.rsqrt(mean_square + norm_eps) * norm_gain


def block_apply(operand, weight):
    blocks = weight.shape[0] // weight.shape[1]
    grouped = operand.reshape(operand.shape[0], blocks, weight.shape[1])
    stacked = weight.reshape(blocks, weight.shape[1], weight.shape[1])
    result = jnp.einsum("rki,kij->rkj", grouped, stacked, preferred_element_type=jnp.float32)
    return result.reshape(operand.shape[0], -1)


def block_back(partner, weight):
    blocks = weight.shape[0] // weight.shape[1]
    grouped = partner.reshape(partner.shape[0], blocks, weight.shape[1])
    stacked = weight.reshape(blocks, weight.shape[1], weight.shape[1])
    result = jnp.einsum("rkj,kij->rki", grouped, stacked, preferred_element_type=jnp.float32)
    return result.reshape(partner.shape[0], -1)


def block_term(operand, partner, blocks, block_size):
    grouped = operand.reshape(operand.shape[0], blocks, block_size)
    other_rows = partner.reshape(partner.shape[0], blocks, block_size)
    result = jnp.einsum("rki,rkj->kij", grouped, other_rows, preferred_element_type=jnp.float32)
    return result.reshape(blocks * block_size, block_size)


def to_columns(row_layout):
    return lax.all_to_all(row_layout, "seq", split_axis=2, concat_axis=1, tiled=True)


def to_rows(col_layout):
    return lax.all_to_all(col_layout, "seq", split_axis=1, concat_axis=2, tiled=True)


def shards_plain(
    inputs,
    norm_gain,
    inner_mix,
    twiddle,
    outer_mix,
    long_kernel,
    gate_weight,
    out_weight,
    cotangent,
):
    batch_local, rows_local, channels = inputs.shape
    inner_len = inner_mix.shape[0]
    local_outer = rows_local // inner_len
    flat_rows = batch_local * rows_local
    block_size = gate_weight.shape[1]
    blocks = gate_weight.shape[0] // block_size
    all_tokens = batch_local * lax.axis_size("dp") * rows_local * lax.axis_size("seq")
    grad_scale = 1.0 / math.sqrt(all_tokens)
    inputs_wide = inputs.reshape(flat_rows, channels).astype(jnp.float32)
    activation = normalize(inputs_wide, norm_gain).astype(jnp.bfloat16)
    grid_rows = activation.reshape(batch_local, local_outer, inner_len, channels)
    inner_out = jnp.einsum(
        "jq,bpqd->bpjd", inner_mix, grid_rows, preferred_element_type=jnp.float32
    )
    mixed_rows = (inner_out * twiddle[None, :, :, None]).astype(jnp.bfloat16)
    columns = to_columns(mixed_rows)
    outer_out = jnp.einsum("ip,bpjd->bijd", outer_mix, columns, preferred_element_type=jnp.float32)
    mixed_cols = (outer_out * long_kernel[None, :, :, None]).astype(jnp.bfloat16)
    seq_mix = to_rows(mixed_cols).reshape(flat_rows, channels)
    gate_pre = block_apply(activation, gate_weight)
    gate_sig = jax.nn.sigmoid(gate_pre)
    mix_wide = seq_mix.astype(jnp.float32)
    gated_rows = (mix_wide * gate_pre * gate_sig).astype(jnp.bfloat16)
    layer_out = (inputs_wide + block_apply(gated_rows, out_weight)).astype(jnp.bfloat16)
    cotan_rows = cotangent.reshape(flat_rows, channels)
    back_gated = block_back(cotan_rows, out_weight)
    mix_grad = (back_gated * gate_pre * gate_sig).astype(jnp.bfloat16)
    gate_grad = (back_gated * mix_wide * gate_sig * (1.0 + gate_pre * (1.0 - gate_sig))).astype(
        jnp.bfloat16
    )
    act_grad = block_back(gate_grad, gate_weight)
    weight_term = jnp.concatenate(
        [
            block_term(activation, gate_grad, blocks, block_size),
            block_term(gated_rows, cotan_rows, blocks, block_size),
        ],
        axis=0,
    )
    grad_cols = to_columns(mix_grad.reshape(batch_local, local_outer, inner_len, channels))
    scaled_back = (grad_cols.astype(jnp.float32) * long_kernel[None, :, :, None]).astype(
        jnp.bfloat16
    )
    back_outer = jnp.einsum(
        "ip,bijd->bpjd", outer_mix, scaled_back, preferred_element_type=jnp.float32
    ).astype(jnp.bfloat16)
    back_rows = to_rows(back_outer)
    twisted = (back_rows.astype(jnp.float32) * twiddle[None, :, :, None]).astype(jnp.bfloat16)
    inner_back = jnp.einsum("jq,bpjd->bpqd", inner_mix, twisted, preferred_element_type=jnp.float32)
    act_grad = act_grad + inner_back.reshape(flat_rows, channels)
    pullback = jax.vjp(lambda wide_rows: normalize(wide_rows, norm_gain), inputs_wide)[1]
    input_grad = (cotan_rows.astype(jnp.float32) + pullback(act_grad)[0]).astype(jnp.bfloat16)
    shard_term = lax.psum_scatter(weight_term, "seq", scatter_dimension=0, tiled=True)
    weight_grads = lax.psum(shard_term, "dp") * grad_scale
    return (layer_out.reshape(inputs.shape), input_grad.reshape(inputs.shape), weight_grads)


def dot(lhs, rhs, lhs_dim=1, rhs_dim=0):
    return lax.dot_general(
        lhs, rhs, (((lhs_dim,), (rhs_dim,)), ((), ())), preferred_element_type=jnp.float32
    )


def row_scale(wide):
    return lax.rsqrt(jnp.sum(wide * wide, axis=-1, keepdims=True) / wide.shape[-1] + norm_eps)


def pick_column(table, at):
    lanes = lax.broadcasted_iota(jnp.int32, table.shape, 1)
    return jnp.sum(jnp.where(lanes == at, table, 0.0), axis=-1, keepdims=True)


def normed(rows, gain):
    wide = rows.astype(jnp.float32)
    return (wide * row_scale(wide) * gain).astype(jnp.bfloat16)


def gate_terms(act, weight):
    gate_pre = dot(act, weight)
    gate_sig = jax.nn.sigmoid(gate_pre)
    return gate_pre, gate_sig


SUB = 16


def leave(x_ref, cot_ref, grad_ref, back_ref, row, twiddle_t_ref, inner_t_ref, gate_ref, gain):
    size = gate_ref.shape[1]
    inner_len, channels = x_ref.shape
    column = pick_column(twiddle_t_ref[...], row)
    parts = []
    for k in range(channels // size):
        part = slice(k * size, (k + 1) * size)
        held = back_ref[:, :, part].reshape(inner_len, size).astype(jnp.float32)
        twisted = (held * column).astype(jnp.bfloat16)
        parts.append(
            dot(grad_ref[:, part], gate_ref[part, :], 1, 1) + dot(inner_t_ref[...], twisted)
        )
    act_grad = jnp.concatenate(parts, axis=1)
    wide = x_ref[...].astype(jnp.float32)
    scale = row_scale(wide)
    pulled = act_grad * gain
    share = jnp.sum(pulled * wide, axis=-1, keepdims=True) / channels
    grad = pulled * scale - wide * (scale * scale * scale * share)
    return (cot_ref[...].astype(jnp.float32) + grad).astype(jnp.bfloat16)


def layer_kernel(
    grad_scale,
    gain_ref,
    inner_ref,
    twiddle_ref,
    outer_ref,
    kernel_ref,
    gate_hbm,
    out_hbm,
    x_hbm,
    cot_hbm,
    weight_buf,
    x_buf,
    cot_buf,
    grad_buf,
    last_buf,
    result_buf,
    gate_buf,
    inner_t_buf,
    twiddle_t_buf,
    gain_buf,
    first_buf,
    second_buf,
    layer_hbm,
    grad_hbm,
    mixed_hbm,
    scaled_hbm,
    seq_hbm,
    back_hbm,
    kernel_buf,
    out_buf,
    wide_outer,
    block_buf,
    swap_buf,
    act_buf,
    term_buf,
    share_buf,
    total_buf,
    piece_buf,
    piece_in_buf,
    far_buf,
    far_in_buf,
    final_buf,
    load_sem,
    store_sem,
    own_sem,
    send_sem,
    in_sem,
    row_sem,
    back_sem,
    back_send_sem,
    layer_sem,
    weight_send_sem,
    weight_sem,
):
    rows, seq_n, cols, channels = first_buf.shape
    dp_n = share_buf.shape[0]
    outer_len = seq_n * rows
    inner_len = seq_n * cols
    size = gate_buf.shape[1]
    blocks = channels // size
    part_cols = block_buf.shape[-1]
    lane_parts = channels // part_cols
    me = lax.axis_index("seq")
    my_dp = lax.axis_index("dp")
    gain = gain_ref[...].reshape(1, channels)
    last = rows - 1
    bf16 = jnp.bfloat16

    def seq_peer(step):
        return lax.rem(me + step, seq_n)

    def dp_peer(step):
        return lax.rem(my_dp + step, dp_n)

    def remote(source, target, send, receive, axis, index):
        return pltpu.make_async_remote_copy(
            src_ref=source,
            dst_ref=target,
            send_sem=send,
            recv_sem=receive,
            device_id={axis: index},
            device_id_type=pl.DeviceIdType.MESH,
        )

    def load(sem, source, target):
        copy = pltpu.make_async_copy(source, target, load_sem.at[sem])
        copy.start()
        return copy

    def store(sem, source, target):
        copy = pltpu.make_async_copy(source, target, store_sem.at[sem])
        copy.start()
        return copy

    def row_send(buf, target, send, receive, row):
        for step in range(1, seq_n):
            peer = seq_peer(step)
            remote(buf.at[row, peer], target.at[me, row], send, receive, "seq", peer).start()

    others = pl.ds(0, seq_n - 1)

    def whole(target, send, receive):
        return remote(target.at[others], target.at[others], send, receive, "seq", seq_peer(1))

    def one_row(target, send, receive, row):
        held = target.at[others, row]
        return remote(held, held, send, receive, "seq", seq_peer(1))

    x_first = load(0, x_hbm.at[0], x_buf)
    weights = [load(2, gate_hbm, gate_buf), load(3, out_hbm, out_buf)]
    twiddle_t_buf[...] = twiddle_ref[...].T
    kernel_buf[...] = kernel_ref[...].T
    gain_buf[...] = gain
    barrier = pltpu.get_barrier_semaphore()
    for step in range(1, seq_n):
        pl.semaphore_signal(
            barrier, 1, device_id={"seq": seq_peer(step)}, device_id_type=pl.DeviceIdType.MESH
        )
    for step in range(1, dp_n):
        pl.semaphore_signal(
            barrier, 1, device_id={"dp": dp_peer(step)}, device_id_type=pl.DeviceIdType.MESH
        )
    def enter_part(row, peer):
        owned = pl.ds(pl.multiple_of(peer * cols, cols), cols)
        mixed = dot(inner_ref[owned, :], act_buf[...])
        first_buf[row, peer] = (mixed * pick_column(twiddle_t_buf[owned, :], row)).astype(bf16)

    def enter_send(row, peer):
        remote(
            first_buf.at[row, peer],
            mixed_hbm.at[me, row],
            send_sem.at[0],
            in_sem.at[0],
            "seq",
            peer,
        ).start()

    def first_part(peer, carry):
        enter_part(0, peer)
        return carry

    x_first.wait()
    act_buf[...] = normed(x_buf[...], gain)
    lax.fori_loop(0, seq_n, first_part, 0)
    pl.semaphore_wait(barrier, seq_n + dp_n - 2)
    row_send(first_buf, mixed_hbm, send_sem.at[0], in_sem.at[0], 0)

    def enter_row(row, carry):
        load(0, x_hbm.at[row], x_buf).wait()
        act_buf[...] = normed(x_buf[...], gain)

        def one_part(step, carry):
            peer = seq_peer(step)
            enter_part(row, peer)

            @pl.when(step < seq_n)
            def _():
                enter_send(row, peer)

            return carry

        lax.fori_loop(1, seq_n + 1, one_part, 0)
        return carry

    lax.fori_loop(1, rows, enter_row, 0)
    mixed_own = pltpu.make_async_copy(first_buf.at[:, me], mixed_hbm.at[me], own_sem.at[0])
    mixed_own.start()

    for copy in weights:
        copy.wait()

    def grad_row(row, carry):
        loads = [load(0, x_hbm.at[row], x_buf), load(1, cot_hbm.at[row], cot_buf)]
        for copy in loads:
            copy.wait()
        act_buf[...] = normed(x_buf[...], gain)

        def one_block(k, carry):
            part = pl.ds(pl.multiple_of(k * size, size), size)
            gate_pre, gate_sig = gate_terms(act_buf[:, part], gate_buf[part, :])
            back = dot(cot_buf[:, part], out_buf[part, :], 1, 1)
            grad = (back * gate_pre * gate_sig).astype(bf16)
            second_buf[row, :, :, part] = grad.reshape(seq_n, cols, size)
            return carry

        lax.fori_loop(0, blocks, one_block, 0)
        row_send(second_buf, scaled_hbm, send_sem.at[1], in_sem.at[1], row)
        return carry

    lax.fori_loop(0, rows, grad_row, 0)
    scaled_own = pltpu.make_async_copy(second_buf.at[:, me], scaled_hbm.at[me], own_sem.at[1])
    scaled_own.start()

    tile = SUB * SUB
    tiles = outer_len // SUB

    def widen_outer(transposed):
        def one(at, carry):
            shape = (tile, outer_len)
            i_of = (lax.broadcasted_iota(jnp.int32, shape, 0) >> 4) + at * SUB
            pick = (i_of == lax.broadcasted_iota(jnp.int32, shape, 1)).astype(bf16)
            picked = dot(pick, outer_ref[...], 1, 1 if transposed else 0).astype(bf16)
            at_row = pl.multiple_of(at * tile, tile)

            def one_part(side, carry):
                shape = (outer_len, tile)
                p_of = (lax.broadcasted_iota(jnp.int32, shape, 1) >> 4) + side * SUB
                spread = (p_of == lax.broadcasted_iota(jnp.int32, shape, 0)).astype(bf16)
                full = dot(picked, spread)
                low = lax.broadcasted_iota(jnp.int32, full.shape, 0) & (SUB - 1)
                high = lax.broadcasted_iota(jnp.int32, full.shape, 1) & (SUB - 1)
                at_lane = pl.multiple_of(side * tile, tile)
                wide_outer[pl.ds(at_row, tile), pl.ds(at_lane, tile)] = jnp.where(
                    low == high, full, 0.0
                ).astype(bf16)
                return carry

            lax.fori_loop(0, tiles, one_part, 0)
            return carry

        lax.fori_loop(0, tiles, one, 0)

    def kernel_column(at, group):
        at_row = pl.multiple_of(at * SUB, SUB)
        table = kernel_buf[pl.ds(at_row, SUB), :]
        spread = jnp.broadcast_to(table[:, None, :], (SUB, SUB, cols)).reshape(tile, cols)
        wanted = (lax.broadcasted_iota(jnp.int32, spread.shape, 0) & (SUB - 1)) + group * SUB
        lanes = lax.broadcasted_iota(jnp.int32, spread.shape, 1)
        return jnp.sum(jnp.where(lanes == wanted, spread, 0.0), axis=-1, keepdims=True)

    tiles_each = rows // SUB

    def mix_outer(source, target, forward):
        def one_block(at, carry):
            group = at // lane_parts
            sub_rows = pl.ds(pl.multiple_of(group * SUB, SUB), SUB)
            lanes = pl.ds(pl.multiple_of((at % lane_parts) * part_cols, part_cols), part_cols)
            load(0, source.at[:, :, sub_rows, lanes], block_buf).wait()

            def whole_of(i):
                return i // tiles_each, pl.ds((i % tiles_each) * SUB, SUB)

            if not forward:

                def scale_tile(i, carry):
                    owner, inside = whole_of(i)
                    held = block_buf[owner, inside].reshape(tile, part_cols).astype(jnp.float32)
                    scaled = (held * kernel_column(i, group)).astype(bf16)
                    block_buf[owner, inside] = scaled.reshape(SUB, SUB, part_cols)
                    return carry

                lax.fori_loop(0, tiles, scale_tile, 0)

            def one_tile(i, carry):
                at_row = pl.multiple_of(i * tile, tile)
                block = block_buf[...].reshape(outer_len * SUB, part_cols)
                mixed = dot(wide_outer[pl.ds(at_row, tile), :], block)
                if forward:
                    mixed = mixed * kernel_column(i, group)
                owner, inside = whole_of(i)
                target[inside, owner, sub_rows, lanes] = mixed.astype(bf16).reshape(
                    SUB, SUB, part_cols
                )
                return carry

            lax.fori_loop(0, tiles, one_tile, 0)
            return carry

        lax.fori_loop(0, cols // SUB * lane_parts, one_block, 0)

    widen_outer(False)
    eye_shape = (inner_len, inner_len)
    eye = lax.broadcasted_iota(jnp.int32, eye_shape, 0) == lax.broadcasted_iota(
        jnp.int32, eye_shape, 1
    )
    inner_t_buf[...] = dot(eye.astype(bf16), inner_ref[...], 1, 1).astype(bf16)

    mixed_own.wait()
    whole(mixed_hbm, send_sem.at[0], in_sem.at[0]).wait()
    mix_outer(mixed_hbm, first_buf, True)

    def seq_send(row, carry):
        row_send(first_buf, seq_hbm, send_sem.at[2], row_sem.at[row], row)
        return carry

    lax.fori_loop(0, rows, seq_send, 0)
    seq_own = pltpu.make_async_copy(first_buf.at[:, me], seq_hbm.at[me], own_sem.at[0])
    seq_own.start()
    widen_outer(True)

    scaled_own.wait()
    whole(scaled_hbm, send_sem.at[1], in_sem.at[1]).wait()
    mix_outer(scaled_hbm, second_buf, False)

    def back_send(row, carry):
        @pl.when(row < last)
        def _():
            row_send(second_buf, back_hbm, back_send_sem.at[row], back_sem.at[row], row)

        @pl.when(row == last)
        def _():
            for step in range(1, seq_n):
                peer = seq_peer(step)
                remote(
                    second_buf.at[row, peer],
                    last_buf.at[me],
                    back_send_sem.at[row],
                    back_sem.at[row],
                    "seq",
                    peer,
                ).start()

        return carry

    last_buf[me] = second_buf[last, me]

    ahead = max(rows // 4, 1)
    lax.fori_loop(0, ahead, back_send, 0)
    back_own = pltpu.make_async_copy(second_buf.at[:, me], back_hbm.at[me], own_sem.at[1])
    back_own.start()

    term_buf[...] = jnp.zeros_like(term_buf)
    seq_own.wait()

    def take_row(source, receive, row):
        one_row(source, send_sem.at[2], receive.at[row], row).wait_recv()
        load(3, source.at[:, row], swap_buf).wait()

    def gate_row(row, carry):
        loads = [load(0, x_hbm.at[row], x_buf), load(1, cot_hbm.at[row], cot_buf)]
        take_row(seq_hbm, row_sem, row)
        for copy in loads:
            copy.wait()
        act_buf[...] = normed(x_buf[...], gain)

        def one_block(k, carry):
            part = pl.ds(pl.multiple_of(k * size, size), size)
            act = act_buf[:, part]
            cot = cot_buf[:, part]
            gate_pre, gate_sig = gate_terms(act, gate_buf[part, :])
            mix = swap_buf[:, :, part].reshape(inner_len, size).astype(jnp.float32)
            gated = (mix * gate_pre * gate_sig).astype(bf16)
            layer = x_buf[:, part].astype(jnp.float32) + dot(gated, out_buf[part, :])
            result_buf[:, :, part] = layer.astype(bf16).reshape(seq_n, cols, size)
            back = dot(cot, out_buf[part, :], 1, 1)
            grad = (back * mix * gate_sig * (1.0 + gate_pre * (1.0 - gate_sig))).astype(bf16)
            grad_buf[:, part] = grad
            held = term_buf.shape[1:]
            term_buf[k] += dot(act, grad, 0, 0).reshape(held)
            term_buf[blocks + k] += dot(gated, cot, 0, 0).reshape(held)
            return carry

        lax.fori_loop(0, blocks, one_block, 0)
        stores = [
            store(0, result_buf, layer_hbm.at[row]),
            store(1, grad_buf, grad_hbm.at[row]),
        ]
        for copy in stores:
            copy.wait()
        return carry

    lax.fori_loop(0, rows, gate_row, 0)

    def share_copy(step):
        peer = dp_peer(step)
        return remote(
            term_buf.at[:, peer],
            share_buf.at[my_dp],
            weight_send_sem.at[0, step],
            weight_sem.at[0, step],
            "dp",
            peer,
        )

    def flipped(step):
        index, bit = me, 1
        while bit <= step:
            if step & bit:
                index = index + bit - 2 * bit * (index // bit % 2)
            bit *= 2
        return index

    bits = [1 << k for k in range(seq_n.bit_length() - 1)]

    def piece_copy(bit, step):
        far = bit == bits[-1]
        return remote(
            far_buf if far else piece_buf.at[step],
            far_in_buf if far else piece_in_buf.at[step],
            weight_send_sem.at[1, step],
            weight_sem.at[1, step],
            "seq",
            flipped(bit),
        )

    def stage_steps(bit):
        return [step for step in range(0, seq_n, bit) if step & bit]

    def send_pieces(bit):
        for step in stage_steps(bit):
            if bit == bits[-1]:
                far_buf[...] = total_buf[step].astype(bf16)
            else:
                piece_buf[step] = total_buf[step]
            piece_copy(bit, step).start()

    def add_pieces(bit):
        for step in stage_steps(bit):
            piece_copy(bit, step).wait()
            landed = far_in_buf[...] if bit == bits[-1] else piece_in_buf[step]
            total_buf[step - bit] += landed.astype(jnp.float32)

    def final_copy(step):
        peer = dp_peer(step)
        return remote(
            final_buf,
            weight_buf.at[my_dp],
            weight_send_sem.at[2, step],
            weight_sem.at[2, step],
            "dp",
            peer,
        )

    for step in range(1, dp_n):
        share_copy(step).start()
    back_own.wait()
    whole(seq_hbm, send_sem.at[2], row_sem.at[0]).wait_send()
    stages = len(bits) + 2
    points = [rows * (k + 1) // (stages + 1) for k in range(stages)]

    def leave_row(row, carry):
        loads = [
            load(0, x_hbm.at[row], x_buf),
            load(1, cot_hbm.at[row], cot_buf),
            load(2, grad_hbm.at[row], grad_buf),
        ]

        @pl.when(row + ahead < rows)
        def _():
            back_send(row + ahead, 0)

        @pl.when(row == points[0])
        def _():
            for step in range(1, dp_n):
                share_copy(step).wait()
            share_buf[my_dp] = term_buf[:, my_dp]
            for step in range(seq_n):
                piece = flipped(step)
                total = share_buf[0, piece]
                for t in range(1, dp_n):
                    total += share_buf[t, piece]
                total_buf[step] = total
            send_pieces(bits[0])

        for stage, bit in enumerate(bits[1:]):

            @pl.when(row == points[stage + 1])
            def _(stage=stage, bit=bit):
                add_pieces(bits[stage])
                send_pieces(bit)

        @pl.when(row == points[len(bits)])
        def _():
            add_pieces(bits[-1])
            final_buf[...] = total_buf[0] * grad_scale
            weight_buf[my_dp] = final_buf[...]
            for step in range(1, dp_n):
                final_copy(step).start()

        for copy in loads:
            copy.wait()
        take_row(back_hbm, back_sem, row)
        one_row(back_hbm, back_send_sem.at[row], back_sem.at[row], row).wait_send()
        layer_row = pltpu.make_async_copy(layer_hbm.at[row], second_buf.at[row], layer_sem)
        layer_row.start()
        result = leave(
            x_buf, cot_buf, grad_buf, swap_buf, row, twiddle_t_buf, inner_t_buf, gate_buf, gain
        )
        first_buf[row] = result.reshape(seq_n, cols, channels)
        layer_row.wait()
        return carry

    lax.fori_loop(0, last, leave_row, 0)
    loads = [
        load(0, x_hbm.at[last], x_buf),
        load(1, cot_hbm.at[last], cot_buf),
        load(2, grad_hbm.at[last], grad_buf),
    ]
    for copy in loads:
        copy.wait()
    for step in range(1, dp_n):
        final_copy(step).wait()
    landed = last_buf.at[others]
    remote(landed, landed, back_send_sem.at[last], back_sem.at[last], "seq", seq_peer(1)).wait()


STORES = 2


def store_kernel(
    weight_ref,
    x_ref,
    cot_ref,
    mid_ref,
    back_ref,
    last_layer_ref,
    gate_ref,
    inner_t_ref,
    twiddle_t_ref,
    gain_ref,
    grad_ref,
    layer_ref,
    layer_hbm,
    input_grad_hbm,
    weight_hbm,
    last_grad_ref,
    sem,
):
    last = grad_ref.shape[0] - 1
    copies = []

    def store(source, target):
        copy = pltpu.make_async_copy(source, target, sem.at[len(copies)])
        copies.append(copy)
        copy.start()

    for k in range(STORES):
        part = pl.ds(k * last // STORES, (k + 1) * last // STORES - k * last // STORES)
        store(layer_ref.at[part], layer_hbm.at[part])
        store(grad_ref.at[part], input_grad_hbm.at[part])
    store(last_layer_ref, layer_hbm.at[last])
    store(weight_ref, weight_hbm)
    result = leave(
        x_ref,
        cot_ref,
        mid_ref,
        back_ref,
        last,
        twiddle_t_ref,
        inner_t_ref,
        gate_ref,
        gain_ref[...],
    )
    last_grad_ref[...] = result.reshape(last_grad_ref.shape)
    store(last_grad_ref, input_grad_hbm.at[last])
    for copy in copies:
        copy.wait()


def shards_fast(
    inputs,
    norm_gain,
    inner_mix,
    twiddle,
    outer_mix,
    long_kernel,
    gate_weight,
    out_weight,
    cotangent,
):
    _, rows_local, channels = inputs.shape
    inner_len = inner_mix.shape[0]
    outer_len = outer_mix.shape[0]
    rows = rows_local // inner_len
    size = gate_weight.shape[1]
    blocks = gate_weight.shape[0] // size
    seq_n = lax.axis_size("seq")
    dp_n = lax.axis_size("dp")
    cols = inner_len // seq_n
    piece = size // dp_n
    grad_scale = 1.0 / math.sqrt(dp_n * rows_local * seq_n)
    bf16 = jnp.bfloat16
    f32 = jnp.float32
    part_cols = channels // 2

    row_shape = jax.ShapeDtypeStruct((rows, inner_len, channels), bf16)
    swap_shape = jax.ShapeDtypeStruct((seq_n, rows, cols, channels), bf16)
    held = pl.BlockSpec(memory_space=pltpu.VMEM)
    anywhere = pl.BlockSpec(memory_space=pl.ANY)
    row_buf = pltpu.VMEM((inner_len, channels), bf16)
    sems = pltpu.SemaphoreType.DMA

    grid_shape = (rows, seq_n, cols, channels)
    piece_row = (seq_n, cols, channels)
    kept = pl.pallas_call(
        functools.partial(layer_kernel, grad_scale),
        in_specs=[held] * 5 + [anywhere] * 4,
        out_specs=[held] * 12 + [anywhere] * 6,
        out_shape=[
            pltpu.VMEM((dp_n, piece, size), f32),
            row_buf,
            row_buf,
            row_buf,
            pltpu.VMEM(piece_row, bf16),
            pltpu.VMEM(piece_row, bf16),
            pltpu.VMEM((blocks * size, size), bf16),
            pltpu.VMEM((inner_len, inner_len), bf16),
            pltpu.VMEM((inner_len, rows), f32),
            pltpu.VMEM((1, channels), f32),
            pltpu.VMEM(grid_shape, bf16),
            pltpu.VMEM(grid_shape, bf16),
            jax.ShapeDtypeStruct(grid_shape, bf16),
            row_shape,
        ]
        + [swap_shape] * 4,
        scratch_shapes=[
            pltpu.VMEM((outer_len, cols), f32),
            pltpu.VMEM((blocks * size, size), bf16),
            pltpu.VMEM((outer_len * SUB, outer_len * SUB), bf16),
            pltpu.VMEM((seq_n, rows, SUB, part_cols), bf16),
            pltpu.VMEM(piece_row, bf16),
            row_buf,
            pltpu.VMEM((seq_n, dp_n, piece, size), f32),
            pltpu.VMEM((dp_n, seq_n, piece, size), f32),
            pltpu.VMEM((seq_n, piece, size), f32),
            pltpu.VMEM((seq_n, piece, size), f32),
            pltpu.VMEM((seq_n, piece, size), f32),
            pltpu.VMEM((piece, size), bf16),
            pltpu.VMEM((piece, size), bf16),
            pltpu.VMEM((piece, size), f32),
            sems((4,)),
            sems((2,)),
            sems((3,)),
            sems((3,)),
            sems((2,)),
            sems((rows,)),
            sems((rows,)),
            sems((rows,)),
            sems,
            sems((3, max(seq_n, dp_n))),
            sems((3, max(seq_n, dp_n))),
        ],
        compiler_params=pltpu.CompilerParams(
            collective_id=0, has_side_effects=True, vmem_limit_bytes=30 * 2**20
        ),
        cost_estimate=pl.CostEstimate(
            flops=24 * rows_local * channels * size,
            bytes_accessed=40 * rows_local * channels,
            transcendentals=0,
        ),
        name="layer",
    )(
        norm_gain,
        inner_mix,
        twiddle,
        outer_mix,
        long_kernel.T,
        gate_weight,
        out_weight,
        inputs.reshape(row_shape.shape),
        cotangent.reshape(row_shape.shape),
    )[:12]
    layer_out, input_grad, weight_grads = pl.pallas_call(
        store_kernel,
        in_specs=[held] * len(kept),
        out_specs=[anywhere] * 3,
        out_shape=[jax.ShapeDtypeStruct(a.shape, a.dtype) for a in (kept[-1], kept[-2], kept[0])],
        scratch_shapes=[pltpu.VMEM(piece_row, bf16), sems((2 * STORES + 3,))],
        compiler_params=pltpu.CompilerParams(vmem_limit_bytes=5 * 2**20),
        name="store",
    )(*kept)
    return (
        layer_out.reshape(inputs.shape),
        input_grad.reshape(inputs.shape),
        weight_grads.reshape(dp_n * piece, size),
    )


def shards(*arrays):
    batch, rows_local, channels = arrays[0].shape
    inner_len = arrays[2].shape[0]
    cols = arrays[5].shape[1]
    size = arrays[6].shape[1]
    blocks = arrays[6].shape[0] // size
    seq_n, dp_n = lax.axis_size("seq"), lax.axis_size("dp")
    fits = (
        batch == 1
        and min(seq_n, dp_n) > 1
        and seq_n & (seq_n - 1) == 0
        and rows_local // inner_len % SUB == 0
        and cols % SUB == 0
        and channels % 256 == 0
        and size % 128 == 0
        and 2 * blocks == seq_n
        and size % (16 * dp_n) == 0
        and inner_len % 128 == 0
    )
    if fits:
        return shards_fast(*arrays)
    return shards_plain(*arrays)


def solution(mesh):
    return jax.shard_map(
        shards,
        mesh=mesh,
        in_specs=(
            P(("groups", "dp"), "seq", None),
            P(),
            P(),
            P("seq", None),
            P(),
            P(None, "seq"),
            P(),
            P(),
            P(("groups", "dp"), "seq", None),
        ),
        out_specs=(
            P(("groups", "dp"), "seq", None),
            P(("groups", "dp"), "seq", None),
            P(("groups", "seq"), None),
        ),
        check_vma=False,
    )
```

```python
import functools
import math

import jax
import jax.numpy as jnp
from jax import lax
from jax.experimental import pallas as pl
from jax.experimental.pallas import tpu as pltpu
from jax.sharding import PartitionSpec as P

norm_eps = 1e-06


def normalize(values, norm_gain):
    mean_square = jnp.mean(values * values, axis=-1, keepdims=True)
    return values * lax.rsqrt(mean_square + norm_eps) * norm_gain


def block_apply(operand, weight):
    blocks = weight.shape[0] // weight.shape[1]
    grouped = operand.reshape(operand.shape[0], blocks, weight.shape[1])
    stacked = weight.reshape(blocks, weight.shape[1], weight.shape[1])
    result = jnp.einsum("rki,kij->rkj", grouped, stacked, preferred_element_type=jnp.float32)
    return result.reshape(operand.shape[0], -1)


def block_back(partner, weight):
    blocks = weight.shape[0] // weight.shape[1]
    grouped = partner.reshape(partner.shape[0], blocks, weight.shape[1])
    stacked = weight.reshape(blocks, weight.shape[1], weight.shape[1])
    result = jnp.einsum("rkj,kij->rki", grouped, stacked, preferred_element_type=jnp.float32)
    return result.reshape(partner.shape[0], -1)


def block_term(operand, partner, blocks, block_size):
    grouped = operand.reshape(operand.shape[0], blocks, block_size)
    other_rows = partner.reshape(partner.shape[0], blocks, block_size)
    result = jnp.einsum("rki,rkj->kij", grouped, other_rows, preferred_element_type=jnp.float32)
    return result.reshape(blocks * block_size, block_size)


def to_columns(row_layout):
    return lax.all_to_all(row_layout, "seq", split_axis=2, concat_axis=1, tiled=True)


def to_rows(col_layout):
    return lax.all_to_all(col_layout, "seq", split_axis=1, concat_axis=2, tiled=True)


def shards_plain(
    inputs,
    norm_gain,
    inner_mix,
    twiddle,
    outer_mix,
    long_kernel,
    gate_weight,
    out_weight,
    cotangent,
):
    batch_local, rows_local, channels = inputs.shape
    inner_len = inner_mix.shape[0]
    local_outer = rows_local // inner_len
    flat_rows = batch_local * rows_local
    block_size = gate_weight.shape[1]
    blocks = gate_weight.shape[0] // block_size
    all_tokens = batch_local * lax.axis_size("dp") * rows_local * lax.axis_size("seq")
    grad_scale = 1.0 / math.sqrt(all_tokens)
    inputs_wide = inputs.reshape(flat_rows, channels).astype(jnp.float32)
    activation = normalize(inputs_wide, norm_gain).astype(jnp.bfloat16)
    grid_rows = activation.reshape(batch_local, local_outer, inner_len, channels)
    inner_out = jnp.einsum(
        "jq,bpqd->bpjd", inner_mix, grid_rows, preferred_element_type=jnp.float32
    )
    mixed_rows = (inner_out * twiddle[None, :, :, None]).astype(jnp.bfloat16)
    columns = to_columns(mixed_rows)
    outer_out = jnp.einsum("ip,bpjd->bijd", outer_mix, columns, preferred_element_type=jnp.float32)
    mixed_cols = (outer_out * long_kernel[None, :, :, None]).astype(jnp.bfloat16)
    seq_mix = to_rows(mixed_cols).reshape(flat_rows, channels)
    gate_pre = block_apply(activation, gate_weight)
    gate_sig = jax.nn.sigmoid(gate_pre)
    mix_wide = seq_mix.astype(jnp.float32)
    gated_rows = (mix_wide * gate_pre * gate_sig).astype(jnp.bfloat16)
    layer_out = (inputs_wide + block_apply(gated_rows, out_weight)).astype(jnp.bfloat16)
    cotan_rows = cotangent.reshape(flat_rows, channels)
    back_gated = block_back(cotan_rows, out_weight)
    mix_grad = (back_gated * gate_pre * gate_sig).astype(jnp.bfloat16)
    gate_grad = (back_gated * mix_wide * gate_sig * (1.0 + gate_pre * (1.0 - gate_sig))).astype(
        jnp.bfloat16
    )
    act_grad = block_back(gate_grad, gate_weight)
    weight_term = jnp.concatenate(
        [
            block_term(activation, gate_grad, blocks, block_size),
            block_term(gated_rows, cotan_rows, blocks, block_size),
        ],
        axis=0,
    )
    grad_cols = to_columns(mix_grad.reshape(batch_local, local_outer, inner_len, channels))
    scaled_back = (grad_cols.astype(jnp.float32) * long_kernel[None, :, :, None]).astype(
        jnp.bfloat16
    )
    back_outer = jnp.einsum(
        "ip,bijd->bpjd", outer_mix, scaled_back, preferred_element_type=jnp.float32
    ).astype(jnp.bfloat16)
    back_rows = to_rows(back_outer)
    twisted = (back_rows.astype(jnp.float32) * twiddle[None, :, :, None]).astype(jnp.bfloat16)
    inner_back = jnp.einsum("jq,bpjd->bpqd", inner_mix, twisted, preferred_element_type=jnp.float32)
    act_grad = act_grad + inner_back.reshape(flat_rows, channels)
    pullback = jax.vjp(lambda wide_rows: normalize(wide_rows, norm_gain), inputs_wide)[1]
    input_grad = (cotan_rows.astype(jnp.float32) + pullback(act_grad)[0]).astype(jnp.bfloat16)
    shard_term = lax.psum_scatter(weight_term, "seq", scatter_dimension=0, tiled=True)
    weight_grads = lax.psum(shard_term, "dp") * grad_scale
    return (layer_out.reshape(inputs.shape), input_grad.reshape(inputs.shape), weight_grads)


def dot(lhs, rhs, lhs_dim=1, rhs_dim=0):
    return lax.dot_general(
        lhs, rhs, (((lhs_dim,), (rhs_dim,)), ((), ())), preferred_element_type=jnp.float32
    )


def row_scale(wide):
    return lax.rsqrt(jnp.sum(wide * wide, axis=-1, keepdims=True) / wide.shape[-1] + norm_eps)


def pick_column(table, at):
    lanes = lax.broadcasted_iota(jnp.int32, table.shape, 1)
    return jnp.sum(jnp.where(lanes == at, table, 0.0), axis=-1, keepdims=True)


def normed(rows, gain):
    wide = rows.astype(jnp.float32)
    return (wide * row_scale(wide) * gain).astype(jnp.bfloat16)


def gate_terms(act, weight):
    gate_pre = dot(act, weight)
    gate_sig = jax.nn.sigmoid(gate_pre)
    return gate_pre, gate_sig


SUB = 16


def leave(x_ref, cot_ref, grad_ref, back_ref, row, twiddle_t_ref, inner_t_ref, gate_ref, gain):
    size = gate_ref.shape[1]
    inner_len, channels = x_ref.shape
    column = pick_column(twiddle_t_ref[...], row)
    parts = []
    for k in range(channels // size):
        part = slice(k * size, (k + 1) * size)
        held = back_ref[:, :, part].reshape(inner_len, size).astype(jnp.float32)
        twisted = (held * column).astype(jnp.bfloat16)
        parts.append(
            dot(grad_ref[:, part], gate_ref[part, :], 1, 1) + dot(inner_t_ref[...], twisted)
        )
    act_grad = jnp.concatenate(parts, axis=1)
    wide = x_ref[...].astype(jnp.float32)
    scale = row_scale(wide)
    pulled = act_grad * gain
    share = jnp.sum(pulled * wide, axis=-1, keepdims=True) / channels
    grad = pulled * scale - wide * (scale * scale * scale * share)
    return (cot_ref[...].astype(jnp.float32) + grad).astype(jnp.bfloat16)


def layer_kernel(
    grad_scale,
    gain_hbm,
    inner_hbm,
    twiddle_hbm,
    outer_hbm,
    kernel_hbm,
    gate_hbm,
    out_hbm,
    x_hbm,
    cot_hbm,
    weight_buf,
    x_buf,
    cot_buf,
    grad_buf,
    last_buf,
    result_buf,
    gate_buf,
    inner_t_buf,
    twiddle_t_buf,
    gain_buf,
    first_buf,
    second_buf,
    layer_hbm,
    grad_hbm,
    mixed_hbm,
    scaled_hbm,
    seq_hbm,
    back_hbm,
    gain_ref,
    inner_ref,
    twiddle_ref,
    outer_ref,
    kernel_ref,
    kernel_buf,
    out_buf,
    wide_outer,
    block_buf,
    swap_buf,
    act_buf,
    term_buf,
    share_buf,
    total_buf,
    piece_buf,
    piece_in_buf,
    far_buf,
    far_in_buf,
    final_buf,
    load_sem,
    store_sem,
    own_sem,
    send_sem,
    in_sem,
    row_sem,
    back_sem,
    back_send_sem,
    layer_sem,
    weight_send_sem,
    weight_sem,
):
    rows, seq_n, cols, channels = first_buf.shape
    dp_n = share_buf.shape[0]
    outer_len = seq_n * rows
    inner_len = seq_n * cols
    size = gate_buf.shape[1]
    blocks = channels // size
    part_cols = block_buf.shape[-1]
    lane_parts = channels // part_cols
    me = lax.axis_index("seq")
    my_dp = lax.axis_index("dp")
    last = rows - 1
    bf16 = jnp.bfloat16

    def seq_peer(step):
        return lax.rem(me + step, seq_n)

    def dp_peer(step):
        return lax.rem(my_dp + step, dp_n)

    def remote(source, target, send, receive, axis, index):
        return pltpu.make_async_remote_copy(
            src_ref=source,
            dst_ref=target,
            send_sem=send,
            recv_sem=receive,
            device_id={axis: index},
            device_id_type=pl.DeviceIdType.MESH,
        )

    def load(sem, source, target):
        copy = pltpu.make_async_copy(source, target, load_sem.at[sem])
        copy.start()
        return copy

    def store(sem, source, target):
        copy = pltpu.make_async_copy(source, target, store_sem.at[sem])
        copy.start()
        return copy

    def row_send(buf, target, send, receive, row):
        for step in range(1, seq_n):
            peer = seq_peer(step)
            remote(buf.at[row, peer], target.at[me, row], send, receive, "seq", peer).start()

    others = pl.ds(0, seq_n - 1)

    def whole(target, send, receive):
        return remote(target.at[others], target.at[others], send, receive, "seq", seq_peer(1))

    def one_row(target, send, receive, row):
        held = target.at[others, row]
        return remote(held, held, send, receive, "seq", seq_peer(1))

    first_loads = [
        load(0, x_hbm.at[0], x_buf),
        load(4, gain_hbm, gain_ref),
        load(5, twiddle_hbm, twiddle_ref),
        load(6, inner_hbm, inner_ref),
    ]
    barrier = pltpu.get_barrier_semaphore()
    for step in range(1, seq_n):
        pl.semaphore_signal(
            barrier, 1, device_id={"seq": seq_peer(step)}, device_id_type=pl.DeviceIdType.MESH
        )
    for step in range(1, dp_n):
        pl.semaphore_signal(
            barrier, 1, device_id={"dp": dp_peer(step)}, device_id_type=pl.DeviceIdType.MESH
        )
    def enter_part(row, peer):
        owned = pl.ds(pl.multiple_of(peer * cols, cols), cols)
        mixed = dot(inner_ref[owned, :], act_buf[...])
        first_buf[row, peer] = (mixed * pick_column(twiddle_t_buf[owned, :], row)).astype(bf16)

    def enter_send(row, peer):
        remote(
            first_buf.at[row, peer],
            mixed_hbm.at[me, row],
            send_sem.at[0],
            in_sem.at[0],
            "seq",
            peer,
        ).start()

    def first_part(peer, carry):
        enter_part(0, peer)
        return carry

    for copy in first_loads:
        copy.wait()
    gain = gain_ref[...].reshape(1, channels)
    twiddle_t_buf[...] = twiddle_ref[...].T
    act_buf[...] = normed(x_buf[...], gain)
    lax.fori_loop(0, seq_n, first_part, 0)
    pl.semaphore_wait(barrier, seq_n + dp_n - 2)
    row_send(first_buf, mixed_hbm, send_sem.at[0], in_sem.at[0], 0)
    weights = [
        load(2, gate_hbm, gate_buf),
        load(3, out_hbm, out_buf),
        load(4, outer_hbm, outer_ref),
        load(5, kernel_hbm, kernel_ref),
    ]
    gain_buf[...] = gain

    def enter_row(row, carry):
        load(0, x_hbm.at[row], x_buf).wait()
        act_buf[...] = normed(x_buf[...], gain)

        def one_part(step, carry):
            peer = seq_peer(step)
            enter_part(row, peer)

            @pl.when(step < seq_n)
            def _():
                enter_send(row, peer)

            return carry

        lax.fori_loop(1, seq_n + 1, one_part, 0)
        return carry

    lax.fori_loop(1, rows, enter_row, 0)
    mixed_own = pltpu.make_async_copy(first_buf.at[:, me], mixed_hbm.at[me], own_sem.at[0])
    mixed_own.start()

    for copy in weights:
        copy.wait()
    kernel_buf[...] = kernel_ref[...].T

    def grad_row(row, carry):
        loads = [load(0, x_hbm.at[row], x_buf), load(1, cot_hbm.at[row], cot_buf)]
        for copy in loads:
            copy.wait()
        act_buf[...] = normed(x_buf[...], gain)

        def one_block(k, carry):
            part = pl.ds(pl.multiple_of(k * size, size), size)
            gate_pre, gate_sig = gate_terms(act_buf[:, part], gate_buf[part, :])
            back = dot(cot_buf[:, part], out_buf[part, :], 1, 1)
            grad = (back * gate_pre * gate_sig).astype(bf16)
            second_buf[row, :, :, part] = grad.reshape(seq_n, cols, size)
            return carry

        lax.fori_loop(0, blocks, one_block, 0)
        row_send(second_buf, scaled_hbm, send_sem.at[1], in_sem.at[1], row)
        return carry

    lax.fori_loop(0, rows, grad_row, 0)
    scaled_own = pltpu.make_async_copy(second_buf.at[:, me], scaled_hbm.at[me], own_sem.at[1])
    scaled_own.start()

    tile = SUB * SUB
    tiles = outer_len // SUB

    def widen_outer(transposed):
        def one(at, carry):
            shape = (tile, outer_len)
            i_of = (lax.broadcasted_iota(jnp.int32, shape, 0) >> 4) + at * SUB
            pick = (i_of == lax.broadcasted_iota(jnp.int32, shape, 1)).astype(bf16)
            picked = dot(pick, outer_ref[...], 1, 1 if transposed else 0).astype(bf16)
            at_row = pl.multiple_of(at * tile, tile)

            def one_part(side, carry):
                shape = (outer_len, tile)
                p_of = (lax.broadcasted_iota(jnp.int32, shape, 1) >> 4) + side * SUB
                spread = (p_of == lax.broadcasted_iota(jnp.int32, shape, 0)).astype(bf16)
                full = dot(picked, spread)
                low = lax.broadcasted_iota(jnp.int32, full.shape, 0) & (SUB - 1)
                high = lax.broadcasted_iota(jnp.int32, full.shape, 1) & (SUB - 1)
                at_lane = pl.multiple_of(side * tile, tile)
                wide_outer[pl.ds(at_row, tile), pl.ds(at_lane, tile)] = jnp.where(
                    low == high, full, 0.0
                ).astype(bf16)
                return carry

            lax.fori_loop(0, tiles, one_part, 0)
            return carry

        lax.fori_loop(0, tiles, one, 0)

    def kernel_column(at, group):
        at_row = pl.multiple_of(at * SUB, SUB)
        table = kernel_buf[pl.ds(at_row, SUB), :]
        spread = jnp.broadcast_to(table[:, None, :], (SUB, SUB, cols)).reshape(tile, cols)
        wanted = (lax.broadcasted_iota(jnp.int32, spread.shape, 0) & (SUB - 1)) + group * SUB
        lanes = lax.broadcasted_iota(jnp.int32, spread.shape, 1)
        return jnp.sum(jnp.where(lanes == wanted, spread, 0.0), axis=-1, keepdims=True)

    tiles_each = rows // SUB

    def mix_outer(source, target, forward):
        def one_block(at, carry):
            group = at // lane_parts
            sub_rows = pl.ds(pl.multiple_of(group * SUB, SUB), SUB)
            lanes = pl.ds(pl.multiple_of((at % lane_parts) * part_cols, part_cols), part_cols)
            load(0, source.at[:, :, sub_rows, lanes], block_buf).wait()

            def whole_of(i):
                return i // tiles_each, pl.ds((i % tiles_each) * SUB, SUB)

            if not forward:

                def scale_tile(i, carry):
                    owner, inside = whole_of(i)
                    held = block_buf[owner, inside].reshape(tile, part_cols).astype(jnp.float32)
                    scaled = (held * kernel_column(i, group)).astype(bf16)
                    block_buf[owner, inside] = scaled.reshape(SUB, SUB, part_cols)
                    return carry

                lax.fori_loop(0, tiles, scale_tile, 0)

            def one_tile(i, carry):
                at_row = pl.multiple_of(i * tile, tile)
                block = block_buf[...].reshape(outer_len * SUB, part_cols)
                mixed = dot(wide_outer[pl.ds(at_row, tile), :], block)
                if forward:
                    mixed = mixed * kernel_column(i, group)
                owner, inside = whole_of(i)
                target[inside, owner, sub_rows, lanes] = mixed.astype(bf16).reshape(
                    SUB, SUB, part_cols
                )
                return carry

            lax.fori_loop(0, tiles, one_tile, 0)
            return carry

        lax.fori_loop(0, cols // SUB * lane_parts, one_block, 0)

    widen_outer(False)
    eye_shape = (inner_len, inner_len)
    eye = lax.broadcasted_iota(jnp.int32, eye_shape, 0) == lax.broadcasted_iota(
        jnp.int32, eye_shape, 1
    )
    inner_t_buf[...] = dot(eye.astype(bf16), inner_ref[...], 1, 1).astype(bf16)

    mixed_own.wait()
    whole(mixed_hbm, send_sem.at[0], in_sem.at[0]).wait()
    mix_outer(mixed_hbm, first_buf, True)

    def seq_send(row, carry):
        row_send(first_buf, seq_hbm, send_sem.at[2], row_sem.at[row], row)
        return carry

    lax.fori_loop(0, rows, seq_send, 0)
    seq_own = pltpu.make_async_copy(first_buf.at[:, me], seq_hbm.at[me], own_sem.at[0])
    seq_own.start()
    widen_outer(True)

    scaled_own.wait()
    whole(scaled_hbm, send_sem.at[1], in_sem.at[1]).wait()
    mix_outer(scaled_hbm, second_buf, False)

    def back_send(row, carry):
        @pl.when(row < last)
        def _():
            row_send(second_buf, back_hbm, back_send_sem.at[row], back_sem.at[row], row)

        @pl.when(row == last)
        def _():
            for step in range(1, seq_n):
                peer = seq_peer(step)
                remote(
                    second_buf.at[row, peer],
                    last_buf.at[me],
                    back_send_sem.at[row],
                    back_sem.at[row],
                    "seq",
                    peer,
                ).start()

        return carry

    last_buf[me] = second_buf[last, me]

    ahead = max(rows // 4, 1)
    lax.fori_loop(0, ahead, back_send, 0)
    back_own = pltpu.make_async_copy(second_buf.at[:, me], back_hbm.at[me], own_sem.at[1])
    back_own.start()

    term_buf[...] = jnp.zeros_like(term_buf)
    seq_own.wait()

    def take_row(source, receive, row):
        one_row(source, send_sem.at[2], receive.at[row], row).wait_recv()
        load(3, source.at[:, row], swap_buf).wait()

    def gate_row(row, carry):
        loads = [load(0, x_hbm.at[row], x_buf), load(1, cot_hbm.at[row], cot_buf)]
        take_row(seq_hbm, row_sem, row)
        for copy in loads:
            copy.wait()
        act_buf[...] = normed(x_buf[...], gain)

        def one_block(k, carry):
            part = pl.ds(pl.multiple_of(k * size, size), size)
            act = act_buf[:, part]
            cot = cot_buf[:, part]
            gate_pre, gate_sig = gate_terms(act, gate_buf[part, :])
            mix = swap_buf[:, :, part].reshape(inner_len, size).astype(jnp.float32)
            gated = (mix * gate_pre * gate_sig).astype(bf16)
            layer = x_buf[:, part].astype(jnp.float32) + dot(gated, out_buf[part, :])
            result_buf[:, :, part] = layer.astype(bf16).reshape(seq_n, cols, size)
            back = dot(cot, out_buf[part, :], 1, 1)
            grad = (back * mix * gate_sig * (1.0 + gate_pre * (1.0 - gate_sig))).astype(bf16)
            grad_buf[:, part] = grad
            held = term_buf.shape[1:]
            term_buf[k] += dot(act, grad, 0, 0).reshape(held)
            term_buf[blocks + k] += dot(gated, cot, 0, 0).reshape(held)
            return carry

        lax.fori_loop(0, blocks, one_block, 0)
        stores = [
            store(0, result_buf, layer_hbm.at[row]),
            store(1, grad_buf, grad_hbm.at[row]),
        ]
        for copy in stores:
            copy.wait()
        return carry

    lax.fori_loop(0, rows, gate_row, 0)

    def share_copy(step):
        peer = dp_peer(step)
        return remote(
            term_buf.at[:, peer],
            share_buf.at[my_dp],
            weight_send_sem.at[0, step],
            weight_sem.at[0, step],
            "dp",
            peer,
        )

    def flipped(step):
        index, bit = me, 1
        while bit <= step:
            if step & bit:
                index = index + bit - 2 * bit * (index // bit % 2)
            bit *= 2
        return index

    bits = [1 << k for k in range(seq_n.bit_length() - 1)]

    def piece_copy(bit, step):
        far = bit == bits[-1]
        return remote(
            far_buf if far else piece_buf.at[step],
            far_in_buf if far else piece_in_buf.at[step],
            weight_send_sem.at[1, step],
            weight_sem.at[1, step],
            "seq",
            flipped(bit),
        )

    def stage_steps(bit):
        return [step for step in range(0, seq_n, bit) if step & bit]

    def send_pieces(bit):
        for step in stage_steps(bit):
            if bit == bits[-1]:
                far_buf[...] = total_buf[step].astype(bf16)
            else:
                piece_buf[step] = total_buf[step]
            piece_copy(bit, step).start()

    def add_pieces(bit):
        for step in stage_steps(bit):
            piece_copy(bit, step).wait()
            landed = far_in_buf[...] if bit == bits[-1] else piece_in_buf[step]
            total_buf[step - bit] += landed.astype(jnp.float32)

    def final_copy(step):
        peer = dp_peer(step)
        return remote(
            final_buf,
            weight_buf.at[my_dp],
            weight_send_sem.at[2, step],
            weight_sem.at[2, step],
            "dp",
            peer,
        )

    for step in range(1, dp_n):
        share_copy(step).start()
    back_own.wait()
    whole(seq_hbm, send_sem.at[2], row_sem.at[0]).wait_send()
    stages = len(bits) + 2
    points = [rows * (k + 1) // (stages + 1) for k in range(stages)]

    def leave_row(row, carry):
        loads = [
            load(0, x_hbm.at[row], x_buf),
            load(1, cot_hbm.at[row], cot_buf),
            load(2, grad_hbm.at[row], grad_buf),
        ]

        @pl.when(row + ahead < rows)
        def _():
            back_send(row + ahead, 0)

        @pl.when(row == points[0])
        def _():
            for step in range(1, dp_n):
                share_copy(step).wait()
            share_buf[my_dp] = term_buf[:, my_dp]
            for step in range(seq_n):
                piece = flipped(step)
                total = share_buf[0, piece]
                for t in range(1, dp_n):
                    total += share_buf[t, piece]
                total_buf[step] = total
            send_pieces(bits[0])

        for stage, bit in enumerate(bits[1:]):

            @pl.when(row == points[stage + 1])
            def _(stage=stage, bit=bit):
                add_pieces(bits[stage])
                send_pieces(bit)

        @pl.when(row == points[len(bits)])
        def _():
            add_pieces(bits[-1])
            final_buf[...] = total_buf[0] * grad_scale
            weight_buf[my_dp] = final_buf[...]
            for step in range(1, dp_n):
                final_copy(step).start()

        for copy in loads:
            copy.wait()
        take_row(back_hbm, back_sem, row)
        one_row(back_hbm, back_send_sem.at[row], back_sem.at[row], row).wait_send()
        layer_row = pltpu.make_async_copy(layer_hbm.at[row], second_buf.at[row], layer_sem)
        layer_row.start()
        result = leave(
            x_buf, cot_buf, grad_buf, swap_buf, row, twiddle_t_buf, inner_t_buf, gate_buf, gain
        )
        first_buf[row] = result.reshape(seq_n, cols, channels)
        layer_row.wait()
        return carry

    lax.fori_loop(0, last, leave_row, 0)
    loads = [
        load(0, x_hbm.at[last], x_buf),
        load(1, cot_hbm.at[last], cot_buf),
        load(2, grad_hbm.at[last], grad_buf),
    ]
    for copy in loads:
        copy.wait()
    for step in range(1, dp_n):
        final_copy(step).wait()
    landed = last_buf.at[others]
    remote(landed, landed, back_send_sem.at[last], back_sem.at[last], "seq", seq_peer(1)).wait()


STORES = 2


def store_kernel(
    weight_ref,
    x_ref,
    cot_ref,
    mid_ref,
    back_ref,
    last_layer_ref,
    gate_ref,
    inner_t_ref,
    twiddle_t_ref,
    gain_ref,
    grad_ref,
    layer_ref,
    layer_hbm,
    input_grad_hbm,
    weight_hbm,
    last_grad_ref,
    sem,
):
    last = grad_ref.shape[0] - 1
    copies = []

    def store(source, target):
        copy = pltpu.make_async_copy(source, target, sem.at[len(copies)])
        copies.append(copy)
        copy.start()

    for k in range(STORES):
        part = pl.ds(k * last // STORES, (k + 1) * last // STORES - k * last // STORES)
        store(layer_ref.at[part], layer_hbm.at[part])
        store(grad_ref.at[part], input_grad_hbm.at[part])
    store(last_layer_ref, layer_hbm.at[last])
    store(weight_ref, weight_hbm)
    result = leave(
        x_ref,
        cot_ref,
        mid_ref,
        back_ref,
        last,
        twiddle_t_ref,
        inner_t_ref,
        gate_ref,
        gain_ref[...],
    )
    last_grad_ref[...] = result.reshape(last_grad_ref.shape)
    store(last_grad_ref, input_grad_hbm.at[last])
    for copy in copies:
        copy.wait()


def shards_fast(
    inputs,
    norm_gain,
    inner_mix,
    twiddle,
    outer_mix,
    long_kernel,
    gate_weight,
    out_weight,
    cotangent,
):
    _, rows_local, channels = inputs.shape
    inner_len = inner_mix.shape[0]
    outer_len = outer_mix.shape[0]
    rows = rows_local // inner_len
    size = gate_weight.shape[1]
    blocks = gate_weight.shape[0] // size
    seq_n = lax.axis_size("seq")
    dp_n = lax.axis_size("dp")
    cols = inner_len // seq_n
    piece = size // dp_n
    grad_scale = 1.0 / math.sqrt(dp_n * rows_local * seq_n)
    bf16 = jnp.bfloat16
    f32 = jnp.float32
    part_cols = channels // 2

    row_shape = jax.ShapeDtypeStruct((rows, inner_len, channels), bf16)
    swap_shape = jax.ShapeDtypeStruct((seq_n, rows, cols, channels), bf16)
    held = pl.BlockSpec(memory_space=pltpu.VMEM)
    anywhere = pl.BlockSpec(memory_space=pl.ANY)
    row_buf = pltpu.VMEM((inner_len, channels), bf16)
    sems = pltpu.SemaphoreType.DMA

    grid_shape = (rows, seq_n, cols, channels)
    piece_row = (seq_n, cols, channels)
    kept = pl.pallas_call(
        functools.partial(layer_kernel, grad_scale),
        in_specs=[anywhere] * 9,
        out_specs=[held] * 12 + [anywhere] * 6,
        out_shape=[
            pltpu.VMEM((dp_n, piece, size), f32),
            row_buf,
            row_buf,
            row_buf,
            pltpu.VMEM(piece_row, bf16),
            pltpu.VMEM(piece_row, bf16),
            pltpu.VMEM((blocks * size, size), bf16),
            pltpu.VMEM((inner_len, inner_len), bf16),
            pltpu.VMEM((inner_len, rows), f32),
            pltpu.VMEM((1, channels), f32),
            pltpu.VMEM(grid_shape, bf16),
            pltpu.VMEM(grid_shape, bf16),
            jax.ShapeDtypeStruct(grid_shape, bf16),
            row_shape,
        ]
        + [swap_shape] * 4,
        scratch_shapes=[
            pltpu.VMEM((channels,), f32),
            pltpu.VMEM((inner_len, inner_len), bf16),
            pltpu.VMEM((rows, inner_len), f32),
            pltpu.VMEM((outer_len, outer_len), bf16),
            pltpu.VMEM((cols, outer_len), f32),
            pltpu.VMEM((outer_len, cols), f32),
            pltpu.VMEM((blocks * size, size), bf16),
            pltpu.VMEM((outer_len * SUB, outer_len * SUB), bf16),
            pltpu.VMEM((seq_n, rows, SUB, part_cols), bf16),
            pltpu.VMEM(piece_row, bf16),
            row_buf,
            pltpu.VMEM((seq_n, dp_n, piece, size), f32),
            pltpu.VMEM((dp_n, seq_n, piece, size), f32),
            pltpu.VMEM((seq_n, piece, size), f32),
            pltpu.VMEM((seq_n, piece, size), f32),
            pltpu.VMEM((seq_n, piece, size), f32),
            pltpu.VMEM((piece, size), bf16),
            pltpu.VMEM((piece, size), bf16),
            pltpu.VMEM((piece, size), f32),
            sems((7,)),
            sems((2,)),
            sems((3,)),
            sems((3,)),
            sems((2,)),
            sems((rows,)),
            sems((rows,)),
            sems((rows,)),
            sems,
            sems((3, max(seq_n, dp_n))),
            sems((3, max(seq_n, dp_n))),
        ],
        compiler_params=pltpu.CompilerParams(
            collective_id=0, has_side_effects=True, vmem_limit_bytes=30 * 2**20
        ),
        cost_estimate=pl.CostEstimate(
            flops=24 * rows_local * channels * size,
            bytes_accessed=40 * rows_local * channels,
            transcendentals=0,
        ),
        name="layer",
    )(
        norm_gain,
        inner_mix,
        twiddle,
        outer_mix,
        long_kernel.T,
        gate_weight,
        out_weight,
        inputs.reshape(row_shape.shape),
        cotangent.reshape(row_shape.shape),
    )[:12]
    layer_out, input_grad, weight_grads = pl.pallas_call(
        store_kernel,
        in_specs=[held] * len(kept),
        out_specs=[anywhere] * 3,
        out_shape=[jax.ShapeDtypeStruct(a.shape, a.dtype) for a in (kept[-1], kept[-2], kept[0])],
        scratch_shapes=[pltpu.VMEM(piece_row, bf16), sems((2 * STORES + 3,))],
        compiler_params=pltpu.CompilerParams(vmem_limit_bytes=5 * 2**20),
        name="store",
    )(*kept)
    return (
        layer_out.reshape(inputs.shape),
        input_grad.reshape(inputs.shape),
        weight_grads.reshape(dp_n * piece, size),
    )


def shards(*arrays):
    batch, rows_local, channels = arrays[0].shape
    inner_len = arrays[2].shape[0]
    cols = arrays[5].shape[1]
    size = arrays[6].shape[1]
    blocks = arrays[6].shape[0] // size
    seq_n, dp_n = lax.axis_size("seq"), lax.axis_size("dp")
    fits = (
        batch == 1
        and min(seq_n, dp_n) > 1
        and seq_n & (seq_n - 1) == 0
        and rows_local // inner_len % SUB == 0
        and cols % SUB == 0
        and channels % 256 == 0
        and size % 128 == 0
        and 2 * blocks == seq_n
        and size % (16 * dp_n) == 0
        and inner_len % 128 == 0
    )
    if fits:
        return shards_fast(*arrays)
    return shards_plain(*arrays)


def solution(mesh):
    return jax.shard_map(
        shards,
        mesh=mesh,
        in_specs=(
            P(("groups", "dp"), "seq", None),
            P(),
            P(),
            P("seq", None),
            P(),
            P(None, "seq"),
            P(),
            P(),
            P(("groups", "dp"), "seq", None),
        ),
        out_specs=(
            P(("groups", "dp"), "seq", None),
            P(("groups", "dp"), "seq", None),
            P(("groups", "seq"), None),
        ),
        check_vma=False,
    )
```

```python
import functools
import math

import jax
import jax.numpy as jnp
from jax import lax
from jax.experimental import pallas as pl
from jax.experimental.pallas import tpu as pltpu
from jax.sharding import PartitionSpec as P

norm_eps = 1e-06


def normalize(values, norm_gain):
    mean_square = jnp.mean(values * values, axis=-1, keepdims=True)
    return values * lax.rsqrt(mean_square + norm_eps) * norm_gain


def block_apply(operand, weight):
    blocks = weight.shape[0] // weight.shape[1]
    grouped = operand.reshape(operand.shape[0], blocks, weight.shape[1])
    stacked = weight.reshape(blocks, weight.shape[1], weight.shape[1])
    result = jnp.einsum("rki,kij->rkj", grouped, stacked, preferred_element_type=jnp.float32)
    return result.reshape(operand.shape[0], -1)


def block_back(partner, weight):
    blocks = weight.shape[0] // weight.shape[1]
    grouped = partner.reshape(partner.shape[0], blocks, weight.shape[1])
    stacked = weight.reshape(blocks, weight.shape[1], weight.shape[1])
    result = jnp.einsum("rkj,kij->rki", grouped, stacked, preferred_element_type=jnp.float32)
    return result.reshape(partner.shape[0], -1)


def block_term(operand, partner, blocks, block_size):
    grouped = operand.reshape(operand.shape[0], blocks, block_size)
    other_rows = partner.reshape(partner.shape[0], blocks, block_size)
    result = jnp.einsum("rki,rkj->kij", grouped, other_rows, preferred_element_type=jnp.float32)
    return result.reshape(blocks * block_size, block_size)


def to_columns(row_layout):
    return lax.all_to_all(row_layout, "seq", split_axis=2, concat_axis=1, tiled=True)


def to_rows(col_layout):
    return lax.all_to_all(col_layout, "seq", split_axis=1, concat_axis=2, tiled=True)


def shards_plain(
    inputs,
    norm_gain,
    inner_mix,
    twiddle,
    outer_mix,
    long_kernel,
    gate_weight,
    out_weight,
    cotangent,
):
    batch_local, rows_local, channels = inputs.shape
    inner_len = inner_mix.shape[0]
    local_outer = rows_local // inner_len
    flat_rows = batch_local * rows_local
    block_size = gate_weight.shape[1]
    blocks = gate_weight.shape[0] // block_size
    all_tokens = batch_local * lax.axis_size("dp") * rows_local * lax.axis_size("seq")
    grad_scale = 1.0 / math.sqrt(all_tokens)
    inputs_wide = inputs.reshape(flat_rows, channels).astype(jnp.float32)
    activation = normalize(inputs_wide, norm_gain).astype(jnp.bfloat16)
    grid_rows = activation.reshape(batch_local, local_outer, inner_len, channels)
    inner_out = jnp.einsum(
        "jq,bpqd->bpjd", inner_mix, grid_rows, preferred_element_type=jnp.float32
    )
    mixed_rows = (inner_out * twiddle[None, :, :, None]).astype(jnp.bfloat16)
    columns = to_columns(mixed_rows)
    outer_out = jnp.einsum("ip,bpjd->bijd", outer_mix, columns, preferred_element_type=jnp.float32)
    mixed_cols = (outer_out * long_kernel[None, :, :, None]).astype(jnp.bfloat16)
    seq_mix = to_rows(mixed_cols).reshape(flat_rows, channels)
    gate_pre = block_apply(activation, gate_weight)
    gate_sig = jax.nn.sigmoid(gate_pre)
    mix_wide = seq_mix.astype(jnp.float32)
    gated_rows = (mix_wide * gate_pre * gate_sig).astype(jnp.bfloat16)
    layer_out = (inputs_wide + block_apply(gated_rows, out_weight)).astype(jnp.bfloat16)
    cotan_rows = cotangent.reshape(flat_rows, channels)
    back_gated = block_back(cotan_rows, out_weight)
    mix_grad = (back_gated * gate_pre * gate_sig).astype(jnp.bfloat16)
    gate_grad = (back_gated * mix_wide * gate_sig * (1.0 + gate_pre * (1.0 - gate_sig))).astype(
        jnp.bfloat16
    )
    act_grad = block_back(gate_grad, gate_weight)
    weight_term = jnp.concatenate(
        [
            block_term(activation, gate_grad, blocks, block_size),
            block_term(gated_rows, cotan_rows, blocks, block_size),
        ],
        axis=0,
    )
    grad_cols = to_columns(mix_grad.reshape(batch_local, local_outer, inner_len, channels))
    scaled_back = (grad_cols.astype(jnp.float32) * long_kernel[None, :, :, None]).astype(
        jnp.bfloat16
    )
    back_outer = jnp.einsum(
        "ip,bijd->bpjd", outer_mix, scaled_back, preferred_element_type=jnp.float32
    ).astype(jnp.bfloat16)
    back_rows = to_rows(back_outer)
    twisted = (back_rows.astype(jnp.float32) * twiddle[None, :, :, None]).astype(jnp.bfloat16)
    inner_back = jnp.einsum("jq,bpjd->bpqd", inner_mix, twisted, preferred_element_type=jnp.float32)
    act_grad = act_grad + inner_back.reshape(flat_rows, channels)
    pullback = jax.vjp(lambda wide_rows: normalize(wide_rows, norm_gain), inputs_wide)[1]
    input_grad = (cotan_rows.astype(jnp.float32) + pullback(act_grad)[0]).astype(jnp.bfloat16)
    shard_term = lax.psum_scatter(weight_term, "seq", scatter_dimension=0, tiled=True)
    weight_grads = lax.psum(shard_term, "dp") * grad_scale
    return (layer_out.reshape(inputs.shape), input_grad.reshape(inputs.shape), weight_grads)


def dot(lhs, rhs, lhs_dim=1, rhs_dim=0):
    return lax.dot_general(
        lhs, rhs, (((lhs_dim,), (rhs_dim,)), ((), ())), preferred_element_type=jnp.float32
    )


def row_scale(wide):
    return lax.rsqrt(jnp.sum(wide * wide, axis=-1, keepdims=True) / wide.shape[-1] + norm_eps)


def pick_column(table, at):
    lanes = lax.broadcasted_iota(jnp.int32, table.shape, 1)
    return jnp.sum(jnp.where(lanes == at, table, 0.0), axis=-1, keepdims=True)


def normed(rows, gain):
    wide = rows.astype(jnp.float32)
    return (wide * row_scale(wide) * gain).astype(jnp.bfloat16)


def gate_terms(act, weight):
    gate_pre = dot(act, weight)
    gate_sig = jax.nn.sigmoid(gate_pre)
    return gate_pre, gate_sig


SUB = 16


def leave(x_ref, cot_ref, grad_ref, back_ref, row, twiddle_t_ref, inner_t_ref, gate_ref, gain):
    size = gate_ref.shape[1]
    inner_len, channels = x_ref.shape
    column = pick_column(twiddle_t_ref[...], row)
    parts = []
    for k in range(channels // size):
        part = slice(k * size, (k + 1) * size)
        held = back_ref[:, :, part].reshape(inner_len, size).astype(jnp.float32)
        twisted = (held * column).astype(jnp.bfloat16)
        parts.append(
            dot(grad_ref[:, part], gate_ref[part, :], 1, 1) + dot(inner_t_ref[...], twisted)
        )
    act_grad = jnp.concatenate(parts, axis=1)
    wide = x_ref[...].astype(jnp.float32)
    scale = row_scale(wide)
    pulled = act_grad * gain
    share = jnp.sum(pulled * wide, axis=-1, keepdims=True) / channels
    grad = pulled * scale - wide * (scale * scale * scale * share)
    return (cot_ref[...].astype(jnp.float32) + grad).astype(jnp.bfloat16)


def layer_kernel(
    grad_scale,
    gain_hbm,
    inner_hbm,
    twiddle_hbm,
    outer_hbm,
    kernel_hbm,
    gate_hbm,
    out_hbm,
    x_hbm,
    cot_hbm,
    weight_buf,
    x_buf,
    cot_buf,
    grad_buf,
    last_buf,
    result_buf,
    gate_buf,
    inner_t_buf,
    twiddle_t_buf,
    gain_buf,
    first_buf,
    second_buf,
    layer_hbm,
    grad_hbm,
    mixed_hbm,
    scaled_hbm,
    seq_hbm,
    back_hbm,
    gain_ref,
    inner_ref,
    twiddle_ref,
    outer_ref,
    kernel_ref,
    kernel_buf,
    out_buf,
    wide_outer,
    block_buf,
    swap_buf,
    act_buf,
    term_buf,
    share_buf,
    total_buf,
    piece_buf,
    piece_in_buf,
    far_buf,
    far_in_buf,
    final_buf,
    load_sem,
    store_sem,
    own_sem,
    send_sem,
    in_sem,
    row_sem,
    back_sem,
    back_send_sem,
    layer_sem,
    weight_send_sem,
    weight_sem,
):
    rows, seq_n, cols, channels = first_buf.shape
    dp_n = share_buf.shape[0]
    outer_len = seq_n * rows
    inner_len = seq_n * cols
    size = gate_buf.shape[1]
    blocks = channels // size
    part_cols = block_buf.shape[-1]
    lane_parts = channels // part_cols
    me = lax.axis_index("seq")
    my_dp = lax.axis_index("dp")
    last = rows - 1
    bf16 = jnp.bfloat16

    def seq_peer(step):
        return lax.rem(me + step, seq_n)

    def dp_peer(step):
        return lax.rem(my_dp + step, dp_n)

    def remote(source, target, send, receive, axis, index):
        return pltpu.make_async_remote_copy(
            src_ref=source,
            dst_ref=target,
            send_sem=send,
            recv_sem=receive,
            device_id={axis: index},
            device_id_type=pl.DeviceIdType.MESH,
        )

    def load(sem, source, target):
        copy = pltpu.make_async_copy(source, target, load_sem.at[sem])
        copy.start()
        return copy

    def store(sem, source, target):
        copy = pltpu.make_async_copy(source, target, store_sem.at[sem])
        copy.start()
        return copy

    def flipped(step):
        index, bit = me, 1
        while bit <= step:
            if step & bit:
                index = index + bit - 2 * bit * (index // bit % 2)
            bit *= 2
        return index

    def row_send(buf, target, send, receive, row):
        for step in reversed(range(1, seq_n)):
            peer = flipped(step)
            remote(buf.at[row, peer], target.at[me, row], send, receive, "seq", peer).start()

    others = pl.ds(0, seq_n - 1)

    def whole(target, send, receive):
        return remote(target.at[others], target.at[others], send, receive, "seq", seq_peer(1))

    def one_row(target, send, receive, row):
        held = target.at[others, row]
        return remote(held, held, send, receive, "seq", seq_peer(1))

    first_loads = [
        load(0, x_hbm.at[0], x_buf),
        load(4, gain_hbm, gain_ref),
        load(5, twiddle_hbm, twiddle_ref),
        load(6, inner_hbm, inner_ref),
    ]
    barrier = pltpu.get_barrier_semaphore()
    for step in range(1, seq_n):
        pl.semaphore_signal(
            barrier, 1, device_id={"seq": seq_peer(step)}, device_id_type=pl.DeviceIdType.MESH
        )
    for step in range(1, dp_n):
        pl.semaphore_signal(
            barrier, 1, device_id={"dp": dp_peer(step)}, device_id_type=pl.DeviceIdType.MESH
        )
    def enter_part(row, peer):
        owned = pl.ds(pl.multiple_of(peer * cols, cols), cols)
        mixed = dot(inner_ref[owned, :], act_buf[...])
        first_buf[row, peer] = (mixed * pick_column(twiddle_t_buf[owned, :], row)).astype(bf16)

    def enter_send(row, peer):
        remote(
            first_buf.at[row, peer],
            mixed_hbm.at[me, row],
            send_sem.at[0],
            in_sem.at[0],
            "seq",
            peer,
        ).start()

    def first_part(peer, carry):
        enter_part(0, peer)
        return carry

    for copy in first_loads:
        copy.wait()
    gain = gain_ref[...].reshape(1, channels)
    twiddle_t_buf[...] = twiddle_ref[...].T
    act_buf[...] = normed(x_buf[...], gain)
    lax.fori_loop(0, seq_n, first_part, 0)
    pl.semaphore_wait(barrier, seq_n + dp_n - 2)
    row_send(first_buf, mixed_hbm, send_sem.at[0], in_sem.at[0], 0)
    weights = [
        load(2, gate_hbm, gate_buf),
        load(3, out_hbm, out_buf),
        load(4, outer_hbm, outer_ref),
        load(5, kernel_hbm, kernel_ref),
    ]
    gain_buf[...] = gain

    def enter_row(row, carry):
        load(0, x_hbm.at[row], x_buf).wait()
        act_buf[...] = normed(x_buf[...], gain)

        def one_part(step, carry):
            peer = seq_peer(step)
            enter_part(row, peer)

            @pl.when(step < seq_n)
            def _():
                enter_send(row, peer)

            return carry

        lax.fori_loop(1, seq_n + 1, one_part, 0)
        return carry

    lax.fori_loop(1, rows, enter_row, 0)
    mixed_own = pltpu.make_async_copy(first_buf.at[:, me], mixed_hbm.at[me], own_sem.at[0])
    mixed_own.start()

    for copy in weights:
        copy.wait()
    kernel_buf[...] = kernel_ref[...].T

    def grad_row(row, carry):
        loads = [load(0, x_hbm.at[row], x_buf), load(1, cot_hbm.at[row], cot_buf)]
        for copy in loads:
            copy.wait()
        act_buf[...] = normed(x_buf[...], gain)

        def one_block(k, carry):
            part = pl.ds(pl.multiple_of(k * size, size), size)
            gate_pre, gate_sig = gate_terms(act_buf[:, part], gate_buf[part, :])
            back = dot(cot_buf[:, part], out_buf[part, :], 1, 1)
            grad = (back * gate_pre * gate_sig).astype(bf16)
            second_buf[row, :, :, part] = grad.reshape(seq_n, cols, size)
            return carry

        lax.fori_loop(0, blocks, one_block, 0)
        row_send(second_buf, scaled_hbm, send_sem.at[1], in_sem.at[1], row)
        return carry

    lax.fori_loop(0, rows, grad_row, 0)
    scaled_own = pltpu.make_async_copy(second_buf.at[:, me], scaled_hbm.at[me], own_sem.at[1])
    scaled_own.start()

    tile = SUB * SUB
    tiles = outer_len // SUB

    def widen_outer(transposed):
        def one(at, carry):
            shape = (tile, outer_len)
            i_of = (lax.broadcasted_iota(jnp.int32, shape, 0) >> 4) + at * SUB
            pick = (i_of == lax.broadcasted_iota(jnp.int32, shape, 1)).astype(bf16)
            picked = dot(pick, outer_ref[...], 1, 1 if transposed else 0).astype(bf16)
            at_row = pl.multiple_of(at * tile, tile)

            def one_part(side, carry):
                shape = (outer_len, tile)
                p_of = (lax.broadcasted_iota(jnp.int32, shape, 1) >> 4) + side * SUB
                spread = (p_of == lax.broadcasted_iota(jnp.int32, shape, 0)).astype(bf16)
                full = dot(picked, spread)
                low = lax.broadcasted_iota(jnp.int32, full.shape, 0) & (SUB - 1)
                high = lax.broadcasted_iota(jnp.int32, full.shape, 1) & (SUB - 1)
                at_lane = pl.multiple_of(side * tile, tile)
                wide_outer[pl.ds(at_row, tile), pl.ds(at_lane, tile)] = jnp.where(
                    low == high, full, 0.0
                ).astype(bf16)
                return carry

            lax.fori_loop(0, tiles, one_part, 0)
            return carry

        lax.fori_loop(0, tiles, one, 0)

    def kernel_column(at, group):
        at_row = pl.multiple_of(at * SUB, SUB)
        table = kernel_buf[pl.ds(at_row, SUB), :]
        spread = jnp.broadcast_to(table[:, None, :], (SUB, SUB, cols)).reshape(tile, cols)
        wanted = (lax.broadcasted_iota(jnp.int32, spread.shape, 0) & (SUB - 1)) + group * SUB
        lanes = lax.broadcasted_iota(jnp.int32, spread.shape, 1)
        return jnp.sum(jnp.where(lanes == wanted, spread, 0.0), axis=-1, keepdims=True)

    tiles_each = rows // SUB

    def mix_outer(source, target, forward):
        def one_block(at, carry):
            group = at // lane_parts
            sub_rows = pl.ds(pl.multiple_of(group * SUB, SUB), SUB)
            lanes = pl.ds(pl.multiple_of((at % lane_parts) * part_cols, part_cols), part_cols)
            load(0, source.at[:, :, sub_rows, lanes], block_buf).wait()

            def whole_of(i):
                return i // tiles_each, pl.ds((i % tiles_each) * SUB, SUB)

            if not forward:

                def scale_tile(i, carry):
                    owner, inside = whole_of(i)
                    held = block_buf[owner, inside].reshape(tile, part_cols).astype(jnp.float32)
                    scaled = (held * kernel_column(i, group)).astype(bf16)
                    block_buf[owner, inside] = scaled.reshape(SUB, SUB, part_cols)
                    return carry

                lax.fori_loop(0, tiles, scale_tile, 0)

            def one_tile(i, carry):
                at_row = pl.multiple_of(i * tile, tile)
                block = block_buf[...].reshape(outer_len * SUB, part_cols)
                mixed = dot(wide_outer[pl.ds(at_row, tile), :], block)
                if forward:
                    mixed = mixed * kernel_column(i, group)
                owner, inside = whole_of(i)
                target[inside, owner, sub_rows, lanes] = mixed.astype(bf16).reshape(
                    SUB, SUB, part_cols
                )
                return carry

            lax.fori_loop(0, tiles, one_tile, 0)
            return carry

        lax.fori_loop(0, cols // SUB * lane_parts, one_block, 0)

    widen_outer(False)
    eye_shape = (inner_len, inner_len)
    eye = lax.broadcasted_iota(jnp.int32, eye_shape, 0) == lax.broadcasted_iota(
        jnp.int32, eye_shape, 1
    )
    inner_t_buf[...] = dot(eye.astype(bf16), inner_ref[...], 1, 1).astype(bf16)

    mixed_own.wait()
    whole(mixed_hbm, send_sem.at[0], in_sem.at[0]).wait()
    mix_outer(mixed_hbm, first_buf, True)

    def seq_send(row, carry):
        row_send(first_buf, seq_hbm, send_sem.at[2], row_sem.at[row], row)
        return carry

    lax.fori_loop(0, rows, seq_send, 0)
    seq_own = pltpu.make_async_copy(first_buf.at[:, me], seq_hbm.at[me], own_sem.at[0])
    seq_own.start()
    widen_outer(True)

    scaled_own.wait()
    whole(scaled_hbm, send_sem.at[1], in_sem.at[1]).wait()
    mix_outer(scaled_hbm, second_buf, False)

    def back_send(row, carry):
        @pl.when(row < last)
        def _():
            row_send(second_buf, back_hbm, back_send_sem.at[row], back_sem.at[row], row)

        @pl.when(row == last)
        def _():
            for step in range(1, seq_n):
                peer = seq_peer(step)
                remote(
                    second_buf.at[row, peer],
                    last_buf.at[me],
                    back_send_sem.at[row],
                    back_sem.at[row],
                    "seq",
                    peer,
                ).start()

        return carry

    last_buf[me] = second_buf[last, me]

    ahead = max(rows // 4, 1)
    lax.fori_loop(0, ahead, back_send, 0)
    back_own = pltpu.make_async_copy(second_buf.at[:, me], back_hbm.at[me], own_sem.at[1])
    back_own.start()

    term_buf[...] = jnp.zeros_like(term_buf)
    seq_own.wait()

    def take_row(source, receive, row):
        one_row(source, send_sem.at[2], receive.at[row], row).wait_recv()
        load(3, source.at[:, row], swap_buf).wait()

    def gate_row(row, carry):
        loads = [load(0, x_hbm.at[row], x_buf), load(1, cot_hbm.at[row], cot_buf)]
        take_row(seq_hbm, row_sem, row)
        for copy in loads:
            copy.wait()
        act_buf[...] = normed(x_buf[...], gain)

        def one_block(k, carry):
            part = pl.ds(pl.multiple_of(k * size, size), size)
            act = act_buf[:, part]
            cot = cot_buf[:, part]
            gate_pre, gate_sig = gate_terms(act, gate_buf[part, :])
            mix = swap_buf[:, :, part].reshape(inner_len, size).astype(jnp.float32)
            gated = (mix * gate_pre * gate_sig).astype(bf16)
            layer = x_buf[:, part].astype(jnp.float32) + dot(gated, out_buf[part, :])
            result_buf[:, :, part] = layer.astype(bf16).reshape(seq_n, cols, size)
            back = dot(cot, out_buf[part, :], 1, 1)
            grad = (back * mix * gate_sig * (1.0 + gate_pre * (1.0 - gate_sig))).astype(bf16)
            grad_buf[:, part] = grad
            held = term_buf.shape[1:]
            term_buf[k] += dot(act, grad, 0, 0).reshape(held)
            term_buf[blocks + k] += dot(gated, cot, 0, 0).reshape(held)
            return carry

        lax.fori_loop(0, blocks, one_block, 0)
        stores = [
            store(0, result_buf, layer_hbm.at[row]),
            store(1, grad_buf, grad_hbm.at[row]),
        ]
        for copy in stores:
            copy.wait()
        return carry

    lax.fori_loop(0, rows, gate_row, 0)

    def share_copy(step):
        peer = dp_peer(step)
        return remote(
            term_buf.at[:, peer],
            share_buf.at[my_dp],
            weight_send_sem.at[0, step],
            weight_sem.at[0, step],
            "dp",
            peer,
        )

    bits = [1 << k for k in range(seq_n.bit_length() - 1)]

    def piece_copy(bit, step):
        far = bit == bits[-1]
        return remote(
            far_buf if far else piece_buf.at[step],
            far_in_buf if far else piece_in_buf.at[step],
            weight_send_sem.at[1, step],
            weight_sem.at[1, step],
            "seq",
            flipped(bit),
        )

    def stage_steps(bit):
        return [step for step in range(0, seq_n, bit) if step & bit]

    def send_pieces(bit):
        for step in stage_steps(bit):
            if bit == bits[-1]:
                far_buf[...] = total_buf[step].astype(bf16)
            else:
                piece_buf[step] = total_buf[step]
            piece_copy(bit, step).start()

    def add_pieces(bit):
        for step in stage_steps(bit):
            piece_copy(bit, step).wait()
            landed = far_in_buf[...] if bit == bits[-1] else piece_in_buf[step]
            total_buf[step - bit] += landed.astype(jnp.float32)

    def final_copy(step):
        peer = dp_peer(step)
        return remote(
            final_buf,
            weight_buf.at[my_dp],
            weight_send_sem.at[2, step],
            weight_sem.at[2, step],
            "dp",
            peer,
        )

    for step in range(1, dp_n):
        share_copy(step).start()
    back_own.wait()
    whole(seq_hbm, send_sem.at[2], row_sem.at[0]).wait_send()
    stages = len(bits) + 2
    points = [rows * (k + 1) // (stages + 1) for k in range(stages)]

    def leave_row(row, carry):
        loads = [
            load(0, x_hbm.at[row], x_buf),
            load(1, cot_hbm.at[row], cot_buf),
            load(2, grad_hbm.at[row], grad_buf),
        ]

        @pl.when(row + ahead < rows)
        def _():
            back_send(row + ahead, 0)

        @pl.when(row == points[0])
        def _():
            for step in range(1, dp_n):
                share_copy(step).wait()
            share_buf[my_dp] = term_buf[:, my_dp]
            for step in range(seq_n):
                piece = flipped(step)
                total = share_buf[0, piece]
                for t in range(1, dp_n):
                    total += share_buf[t, piece]
                total_buf[step] = total
            send_pieces(bits[0])

        for stage, bit in enumerate(bits[1:]):

            @pl.when(row == points[stage + 1])
            def _(stage=stage, bit=bit):
                add_pieces(bits[stage])
                send_pieces(bit)

        @pl.when(row == points[len(bits)])
        def _():
            add_pieces(bits[-1])
            final_buf[...] = total_buf[0] * grad_scale
            weight_buf[my_dp] = final_buf[...]
            for step in range(1, dp_n):
                final_copy(step).start()

        for copy in loads:
            copy.wait()
        take_row(back_hbm, back_sem, row)
        one_row(back_hbm, back_send_sem.at[row], back_sem.at[row], row).wait_send()
        layer_row = pltpu.make_async_copy(layer_hbm.at[row], second_buf.at[row], layer_sem)
        layer_row.start()
        result = leave(
            x_buf, cot_buf, grad_buf, swap_buf, row, twiddle_t_buf, inner_t_buf, gate_buf, gain
        )
        first_buf[row] = result.reshape(seq_n, cols, channels)
        layer_row.wait()
        return carry

    lax.fori_loop(0, last, leave_row, 0)
    loads = [
        load(0, x_hbm.at[last], x_buf),
        load(1, cot_hbm.at[last], cot_buf),
        load(2, grad_hbm.at[last], grad_buf),
    ]
    for copy in loads:
        copy.wait()
    for step in range(1, dp_n):
        final_copy(step).wait()
    landed = last_buf.at[others]
    remote(landed, landed, back_send_sem.at[last], back_sem.at[last], "seq", seq_peer(1)).wait()


STORES = 2


def store_kernel(
    weight_ref,
    x_ref,
    cot_ref,
    mid_ref,
    back_ref,
    last_layer_ref,
    gate_ref,
    inner_t_ref,
    twiddle_t_ref,
    gain_ref,
    grad_ref,
    layer_ref,
    layer_hbm,
    input_grad_hbm,
    weight_hbm,
    last_grad_ref,
    sem,
):
    last = grad_ref.shape[0] - 1
    copies = []

    def store(source, target):
        copy = pltpu.make_async_copy(source, target, sem.at[len(copies)])
        copies.append(copy)
        copy.start()

    for k in range(STORES):
        part = pl.ds(k * last // STORES, (k + 1) * last // STORES - k * last // STORES)
        store(layer_ref.at[part], layer_hbm.at[part])
        store(grad_ref.at[part], input_grad_hbm.at[part])
    store(last_layer_ref, layer_hbm.at[last])
    store(weight_ref, weight_hbm)
    result = leave(
        x_ref,
        cot_ref,
        mid_ref,
        back_ref,
        last,
        twiddle_t_ref,
        inner_t_ref,
        gate_ref,
        gain_ref[...],
    )
    last_grad_ref[...] = result.reshape(last_grad_ref.shape)
    store(last_grad_ref, input_grad_hbm.at[last])
    for copy in copies:
        copy.wait()


def shards_fast(
    inputs,
    norm_gain,
    inner_mix,
    twiddle,
    outer_mix,
    long_kernel,
    gate_weight,
    out_weight,
    cotangent,
):
    _, rows_local, channels = inputs.shape
    inner_len = inner_mix.shape[0]
    outer_len = outer_mix.shape[0]
    rows = rows_local // inner_len
    size = gate_weight.shape[1]
    blocks = gate_weight.shape[0] // size
    seq_n = lax.axis_size("seq")
    dp_n = lax.axis_size("dp")
    cols = inner_len // seq_n
    piece = size // dp_n
    grad_scale = 1.0 / math.sqrt(dp_n * rows_local * seq_n)
    bf16 = jnp.bfloat16
    f32 = jnp.float32
    part_cols = channels // 2

    row_shape = jax.ShapeDtypeStruct((rows, inner_len, channels), bf16)
    swap_shape = jax.ShapeDtypeStruct((seq_n, rows, cols, channels), bf16)
    held = pl.BlockSpec(memory_space=pltpu.VMEM)
    anywhere = pl.BlockSpec(memory_space=pl.ANY)
    row_buf = pltpu.VMEM((inner_len, channels), bf16)
    sems = pltpu.SemaphoreType.DMA

    grid_shape = (rows, seq_n, cols, channels)
    piece_row = (seq_n, cols, channels)
    kept = pl.pallas_call(
        functools.partial(layer_kernel, grad_scale),
        in_specs=[anywhere] * 9,
        out_specs=[held] * 12 + [anywhere] * 6,
        out_shape=[
            pltpu.VMEM((dp_n, piece, size), f32),
            row_buf,
            row_buf,
            row_buf,
            pltpu.VMEM(piece_row, bf16),
            pltpu.VMEM(piece_row, bf16),
            pltpu.VMEM((blocks * size, size), bf16),
            pltpu.VMEM((inner_len, inner_len), bf16),
            pltpu.VMEM((inner_len, rows), f32),
            pltpu.VMEM((1, channels), f32),
            pltpu.VMEM(grid_shape, bf16),
            pltpu.VMEM(grid_shape, bf16),
            jax.ShapeDtypeStruct(grid_shape, bf16),
            row_shape,
        ]
        + [swap_shape] * 4,
        scratch_shapes=[
            pltpu.VMEM((channels,), f32),
            pltpu.VMEM((inner_len, inner_len), bf16),
            pltpu.VMEM((rows, inner_len), f32),
            pltpu.VMEM((outer_len, outer_len), bf16),
            pltpu.VMEM((cols, outer_len), f32),
            pltpu.VMEM((outer_len, cols), f32),
            pltpu.VMEM((blocks * size, size), bf16),
            pltpu.VMEM((outer_len * SUB, outer_len * SUB), bf16),
            pltpu.VMEM((seq_n, rows, SUB, part_cols), bf16),
            pltpu.VMEM(piece_row, bf16),
            row_buf,
            pltpu.VMEM((seq_n, dp_n, piece, size), f32),
            pltpu.VMEM((dp_n, seq_n, piece, size), f32),
            pltpu.VMEM((seq_n, piece, size), f32),
            pltpu.VMEM((seq_n, piece, size), f32),
            pltpu.VMEM((seq_n, piece, size), f32),
            pltpu.VMEM((piece, size), bf16),
            pltpu.VMEM((piece, size), bf16),
            pltpu.VMEM((piece, size), f32),
            sems((7,)),
            sems((2,)),
            sems((3,)),
            sems((3,)),
            sems((2,)),
            sems((rows,)),
            sems((rows,)),
            sems((rows,)),
            sems,
            sems((3, max(seq_n, dp_n))),
            sems((3, max(seq_n, dp_n))),
        ],
        compiler_params=pltpu.CompilerParams(
            collective_id=0, has_side_effects=True, vmem_limit_bytes=30 * 2**20
        ),
        cost_estimate=pl.CostEstimate(
            flops=24 * rows_local * channels * size,
            bytes_accessed=40 * rows_local * channels,
            transcendentals=0,
        ),
        name="layer",
    )(
        norm_gain,
        inner_mix,
        twiddle,
        outer_mix,
        long_kernel.T,
        gate_weight,
        out_weight,
        inputs.reshape(row_shape.shape),
        cotangent.reshape(row_shape.shape),
    )[:12]
    layer_out, input_grad, weight_grads = pl.pallas_call(
        store_kernel,
        in_specs=[held] * len(kept),
        out_specs=[anywhere] * 3,
        out_shape=[jax.ShapeDtypeStruct(a.shape, a.dtype) for a in (kept[-1], kept[-2], kept[0])],
        scratch_shapes=[pltpu.VMEM(piece_row, bf16), sems((2 * STORES + 3,))],
        compiler_params=pltpu.CompilerParams(vmem_limit_bytes=5 * 2**20),
        name="store",
    )(*kept)
    return (
        layer_out.reshape(inputs.shape),
        input_grad.reshape(inputs.shape),
        weight_grads.reshape(dp_n * piece, size),
    )


def shards(*arrays):
    batch, rows_local, channels = arrays[0].shape
    inner_len = arrays[2].shape[0]
    cols = arrays[5].shape[1]
    size = arrays[6].shape[1]
    blocks = arrays[6].shape[0] // size
    seq_n, dp_n = lax.axis_size("seq"), lax.axis_size("dp")
    fits = (
        batch == 1
        and min(seq_n, dp_n) > 1
        and seq_n & (seq_n - 1) == 0
        and rows_local // inner_len % SUB == 0
        and cols % SUB == 0
        and channels % 256 == 0
        and size % 128 == 0
        and 2 * blocks == seq_n
        and size % (16 * dp_n) == 0
        and inner_len % 128 == 0
    )
    if fits:
        return shards_fast(*arrays)
    return shards_plain(*arrays)


def solution(mesh):
    return jax.shard_map(
        shards,
        mesh=mesh,
        in_specs=(
            P(("groups", "dp"), "seq", None),
            P(),
            P(),
            P("seq", None),
            P(),
            P(None, "seq"),
            P(),
            P(),
            P(("groups", "dp"), "seq", None),
        ),
        out_specs=(
            P(("groups", "dp"), "seq", None),
            P(("groups", "dp"), "seq", None),
            P(("groups", "seq"), None),
        ),
        check_vma=False,
    )
```
